128 devices in a mesh: lat: 4 (over z), lon: 32 (over x, y, core).
Axes of the slice: x: 4, y: 4, z: 4, core: 2. Of those that a mesh axis runs over, the one named last changes fastest.
Arguments:
- grid_lat: bfloat16 [131072, 512], P(('lat', 'lon')), may hold values from -6 to 6
- mesh_lat: bfloat16 [8192, 512], P(('lat', 'lon')), may hold values from -6 to 6
- g2m_send: int32 [128, 9, 256], P(('lat', 'lon')), may hold values from -1 to 1023, as said below
- g2m_recv: int32 [128, 9, 256], P(('lat', 'lon')), may hold values from -1 to 63, as said below
- g2m_feat: bfloat16 [128, 4, 2304], P(('lat', 'lon')), may hold values from -6 to 6
- halo_lists: int32 [128, 4, 16], P(('lat', 'lon')), may hold values from 0 to 63
- proc_send: int32 [128, 512], P(('lat', 'lon')), may hold values from 0 to 127, as said below
- proc_recv: int32 [128, 512], P(('lat', 'lon')), may hold values from 0 to 63
- cotangent: bfloat16 [8192, 512], P(('lat', 'lon')), may hold values from -6 to 6
- w_grid_send: bfloat16 [512, 512], replicated, may hold values from -0.25 to 0.25
- w_grid_recv: bfloat16 [512, 512], replicated, may hold values from -0.25 to 0.25
- w_grid_feat: bfloat16 [4, 512], replicated, may hold values from -3 to 3
- w_grid_out: bfloat16 [512, 512], replicated, may hold values from -0.25 to 0.25
- gain_grid: float32 [512], replicated, may hold values from 0.5 to 1.5
- w_node_in: bfloat16 [1024, 512], replicated, may hold values from -0.1875 to 0.1875
- w_node_out: bfloat16 [512, 512], replicated, may hold values from -0.25 to 0.25
- gain_node: float32 [512], replicated, may hold values from 0.5 to 1.5
- w_proc_send: bfloat16 [512, 512], replicated, may hold values from -0.25 to 0.25
- w_proc_recv: bfloat16 [512, 512], replicated, may hold values from -0.25 to 0.25
- w_proc_out: bfloat16 [512, 512], replicated, may hold values from -0.25 to 0.25
- gain_proc: float32 [512], replicated, may hold values from 0.5 to 1.5
- w_upd_in: bfloat16 [1024, 512], replicated, may hold values from -0.1875 to 0.1875
- w_upd_out: bfloat16 [512, 512], replicated, may hold values from -0.25 to 0.25
- gain_upd: float32 [512], replicated, may hold values from 0.5 to 1.5
Outputs:
- mesh_out: float32 [8192, 512], P(('lat', 'lon'))
- grid_grad: float32 [131072, 512], P(('lat', 'lon'))
- grad_grid_send: float32 [512, 512], replicated
- grad_grid_recv: float32 [512, 512], replicated
- grad_grid_out: float32 [512, 512], replicated
- grad_proc_send: float32 [512, 512], replicated
- grad_proc_recv: float32 [512, 512], replicated
- grad_proc_out: float32 [512, 512], replicated
The draws below stay inside these ranges and needn't reach their ends.
Inputs may be any that keep to these rules, and one draw needn't show every extreme that they name: `g2m_send`: row within source device s's 1024 grid rows of the sender of slot c from s to the owner (a + dlat, (b + dlon) mod 32) at offset k, or -1 for an unused slot. Slot (s, k, c) is used exactly when the owner's g2m_recv[o, k, c] is; offsets that leave the lat range are never used; in every draw some owner's slots are full from every source that exists. `g2m_recv`: row within owner o's 64 mesh rows of the receiver of slot c from the source at offset k below o, or -1 for an unused slot. `proc_send`: row of device p's sender table: own rows first, then the blocks from lat below, lat above, lon below, lon above. Devices at lat index 0 never name the block from below, those at the last lat index never the block from above.
All inputs are finite; a program needn't handle non-finite values.
Results may differ from the reference program's by a relative error of at most 0.018.
Values may be sent and summed in bfloat16 or wider, within the bound.
A program may use at most 128 MiB of HBM per device.

```python
import jax
import jax.numpy as jnp
from jax import lax

L = 512
EF = 4
GD = 1024
MD = 64
CAP = 256
HC = 16
ME = 512
NG = 131072
NM = 8192
N_LAT = 4
N_LON = 32
DEVICES = 128


def g2m_tables(key):
    base = jax.random.fold_in(key, 7177)
    keys = jax.random.split(base, 5)
    devices = N_LAT * N_LON
    owners = jnp.arange(devices, dtype=jnp.int32)
    offsets = jnp.arange(9, dtype=jnp.int32)
    off_lat = offsets // 3 - 1
    off_lon = offsets % 3 - 1
    lat_of = owners // N_LON
    lon_of = owners % N_LON
    levels = 2 ** jax.random.randint(keys[0], (devices,), 0, 4)
    fullest = jax.random.randint(keys[1], (), 0, devices)
    levels = jnp.where(owners == fullest, 8, levels)
    coins = jax.random.randint(keys[2], (devices, 9, CAP), 0, 8)
    src_lat = lat_of[:, None] - off_lat[None, :]
    src_ok = (src_lat >= 0) & (src_lat < N_LAT)
    used_recv = (coins < levels[:, None, None]) & src_ok[:, :, None]
    target_rows = jax.random.randint(keys[4], (devices, 9, CAP), 0, MD)
    receivers = jnp.where(used_recv, target_rows, -1)
    dst_lat = lat_of[:, None] + off_lat[None, :]
    dst_ok = (dst_lat >= 0) & (dst_lat < N_LAT)
    dst_dev = (jnp.clip(dst_lat, 0, N_LAT - 1) * N_LON + (lon_of[:, None] + off_lon[None, :]) % N_LON).astype(jnp.int32)
    used_send = dst_ok[:, :, None] & used_recv[dst_dev, jnp.broadcast_to(offsets[None, :], dst_dev.shape), :]
    source_rows = jax.random.randint(keys[3], (devices, 9, CAP), 0, GD)
    senders = jnp.where(used_send, source_rows, -1)
    return (senders.astype(jnp.int32), receivers.astype(jnp.int32))


def draw_g2m_send(key, part):
    return g2m_tables(key)[0]


def draw_g2m_recv(key, part):
    return g2m_tables(key)[1]


def draw_proc_send(key, part):
    devices = N_LAT * N_LON
    drawn = jax.random.randint(jax.random.fold_in(key, 9011), (devices, ME), 0, MD + 4 * HC)
    lat_index = (jnp.arange(devices) // N_LON)[:, None]
    lowest = (lat_index == 0) & (drawn >= MD) & (drawn < MD + HC)
    highest = (lat_index == N_LAT - 1) & (drawn >= MD + HC) & (drawn < MD + 2 * HC)
    result = jnp.where(lowest, drawn - MD, jnp.where(highest, drawn - MD - HC, drawn))
    return result.astype(jnp.int32)


def with_ends(array, stream_key, smallest, largest):
    index_at = [jax.random.randint(jax.random.fold_in(stream_key, axis), (), 0, length) for axis, length in enumerate(array.shape)]
    longest = array.shape.index(max(array.shape))
    next_to = index_at[:longest] + [(index_at[longest] + 1) % array.shape[longest]] + index_at[longest + 1:]
    return array.at[tuple(index_at)].set(smallest).at[tuple(next_to)].set(largest)


def shard_levels(own_key, dims, pieces, smallest, largest):
    def one(dim, parts):
        draws = jax.random.uniform(jax.random.fold_in(jax.random.fold_in(own_key, 6), dim), (parts,), jnp.float32, smallest / len(pieces), largest / len(pieces))
        return jnp.repeat(jnp.exp(draws), dims[dim] // parts).reshape((-1,) + (1,) * (len(dims) - dim - 1))

    factor_of = one(*pieces[0])
    for cut in pieces[1:]:
        factor_of = factor_of * one(*cut)
    return factor_of


def normal_values(stream_key, extent, deviation, reach, cuts=(), held_as=jnp.bfloat16):
    loudness = shard_levels(stream_key, extent, cuts, -0.22, 0.18) if cuts else 1.0
    values = jax.random.normal(stream_key, extent, jnp.float32) * deviation * loudness
    return jnp.minimum(jnp.maximum(values, -reach), reach).astype(held_as)


def setup_inputs(seed: int = 0) -> dict:
    arg_keys = jax.random.split(jax.random.key(seed), 25)
    return {
        "grid_lat": normal_values(arg_keys[0], (NG, L), 1.0, 6.0, ((0, 128),)),
        "mesh_lat": normal_values(arg_keys[1], (NM, L), 1.0, 6.0, ((0, 128),)),
        "g2m_send": draw_g2m_send(jax.random.fold_in(arg_keys[24], 71), 0),
        "g2m_recv": draw_g2m_recv(jax.random.fold_in(arg_keys[24], 71), 0),
        "g2m_feat": normal_values(arg_keys[4], (DEVICES, EF, 9 * CAP), 1.0, 6.0, ((0, 128),)),
        "halo_lists": with_ends(jax.random.randint(arg_keys[5], (DEVICES, 4, HC), 0, MD), jax.random.fold_in(arg_keys[5], 1), 0, MD - 1).astype(jnp.int32),
        "proc_send": draw_proc_send(jax.random.fold_in(arg_keys[24], 71), 0),
        "proc_recv": with_ends(jax.random.randint(arg_keys[7], (DEVICES, ME), 0, MD), jax.random.fold_in(arg_keys[7], 1), 0, MD - 1).astype(jnp.int32),
        "cotangent": normal_values(arg_keys[8], (NM, L), 1.0, 6.0, ((0, 128),)),
        "w_grid_send": normal_values(arg_keys[9], (L, L), L ** -0.5, 0.25),
        "w_grid_recv": normal_values(arg_keys[10], (L, L), L ** -0.5, 0.25),
        "w_grid_feat": normal_values(arg_keys[11], (EF, L), EF ** -0.5, 3.0),
        "w_grid_out": normal_values(arg_keys[12], (L, L), L ** -0.5, 0.25),
        "gain_grid": jnp.clip(1.0 + 0.1 * jax.random.normal(arg_keys[13], (L,), jnp.float32), 0.5, 1.5),
        "w_node_in": normal_values(arg_keys[14], (2 * L, L), (2 * L) ** -0.5, 0.1875),
        "w_node_out": normal_values(arg_keys[15], (L, L), L ** -0.5, 0.25),
        "gain_node": jnp.clip(1.0 + 0.1 * jax.random.normal(arg_keys[16], (L,), jnp.float32), 0.5, 1.5),
        "w_proc_send": normal_values(arg_keys[17], (L, L), L ** -0.5, 0.25),
        "w_proc_recv": normal_values(arg_keys[18], (L, L), L ** -0.5, 0.25),
        "w_proc_out": normal_values(arg_keys[19], (L, L), L ** -0.5, 0.25),
        "gain_proc": jnp.clip(1.0 + 0.1 * jax.random.normal(arg_keys[20], (L,), jnp.float32), 0.5, 1.5),
        "w_upd_in": normal_values(arg_keys[21], (2 * L, L), (2 * L) ** -0.5, 0.1875),
        "w_upd_out": normal_values(arg_keys[22], (L, L), L ** -0.5, 0.25),
        "gain_upd": jnp.clip(1.0 + 0.1 * jax.random.normal(arg_keys[23], (L,), jnp.float32), 0.5, 1.5),
    }


EPSILON = 1e-05

def inner_rows(matrix_one, matrix_two, precision=None):
    return lax.dot_general(matrix_one, matrix_two, (((0,), (0,)), ((), ())), precision=precision, preferred_element_type=jnp.float32)

def outer_cols(matrix_one, matrix_two):
    return lax.dot_general(matrix_one, matrix_two, (((1,), (1,)), ((), ())), preferred_element_type=jnp.float32)

def tail_forward(preact, weight_out, gain_vec):
    sigmoid_act = jax.nn.sigmoid(preact)
    hidden = (preact * sigmoid_act).astype(jnp.bfloat16)
    mixed_out = jnp.dot(hidden, weight_out, preferred_element_type=jnp.float32)
    centre = mixed_out - lax.optimization_barrier(jnp.mean(mixed_out, axis=-1, keepdims=True))
    inv_std = lax.rsqrt(lax.optimization_barrier(jnp.mean(centre * centre, axis=-1, keepdims=True)) + EPSILON)
    normed = centre * inv_std
    return (normed * gain_vec, (sigmoid_act, hidden, normed, inv_std))

def tail_backward(preact, stash, grad_out, weight_out, gain_vec):
    sigmoid_act, hidden, normed, inv_std = stash
    upstream = grad_out * gain_vec
    grad_mixed = inv_std * (upstream - lax.optimization_barrier(jnp.mean(upstream, axis=-1, keepdims=True)) - normed * lax.optimization_barrier(jnp.mean(upstream * normed, axis=-1, keepdims=True)))
    grad_mixed = grad_mixed.astype(jnp.bfloat16)
    weight_grad = inner_rows(hidden, grad_mixed)
    grad_hidden = outer_cols(grad_mixed, weight_out)
    slope = sigmoid_act + preact * sigmoid_act * (1.0 - sigmoid_act)
    return (grad_hidden * slope, weight_grad)

def take_rows(table, index):
    return jnp.take(table, index, axis=0)

def reference(grid_lat, mesh_lat, g2m_send, g2m_recv, g2m_feat, halo_lists, proc_send, proc_recv, cotangent, w_grid_send, w_grid_recv, w_grid_feat, w_grid_out, gain_grid, w_node_in, w_node_out, gain_node, w_proc_send, w_proc_recv, w_proc_out, gain_proc, w_upd_in, w_upd_out, gain_upd):
    devices = N_LAT * N_LON
    owners = jnp.arange(devices, dtype=jnp.int32)
    offsets = jnp.arange(9, dtype=jnp.int32)
    off_lat = offsets // 3 - 1
    off_lon = offsets % 3 - 1
    lat_of = owners // N_LON
    lon_of = owners % N_LON
    src_lat = lat_of[:, None] - off_lat[None, :]
    src_ok = (src_lat >= 0) & (src_lat < N_LAT)
    src_dev = (jnp.clip(src_lat, 0, N_LAT - 1) * N_LON + (lon_of[:, None] - off_lon[None, :]) % N_LON).astype(jnp.int32)
    grid_terms = jnp.dot(grid_lat, w_grid_send, preferred_element_type=jnp.float32).reshape(devices, GD, L)
    recv_terms = jnp.dot(mesh_lat, w_grid_recv, preferred_element_type=jnp.float32).reshape(devices, MD, L)
    mesh_blocks = mesh_lat.reshape(devices, MD, L)

    def owner_pre(owner_dev):
        sources = src_dev[owner_dev]
        senders = g2m_send[sources, offsets, :]
        sender_ok = src_ok[owner_dev][:, None] & (senders >= 0)
        sender_idx = jnp.maximum(senders, 0)
        picked = grid_terms[sources[:, None], sender_idx]
        slots = jnp.where(sender_ok[:, :, None], picked, 0.0).astype(jnp.bfloat16).reshape(9 * CAP, L)
        receivers = g2m_recv[owner_dev].reshape(-1)
        recv_ok = (receivers >= 0).astype(jnp.float32)
        recv_idx = jnp.maximum(receivers, 0)
        edge_terms = inner_rows(g2m_feat[owner_dev], w_grid_feat)
        preact = slots.astype(jnp.float32) + jnp.take(recv_terms[owner_dev], recv_idx, axis=0) + edge_terms
        return (preact, recv_idx, recv_ok, sources, sender_idx, sender_ok)

    def owner_forward(owner_dev):
        preact, recv_idx, recv_ok, sources, sender_idx, sender_ok = owner_pre(owner_dev)
        message, stash = tail_forward(preact, w_grid_out, gain_grid)
        return jax.ops.segment_sum(message * recv_ok[:, None], recv_idx, num_segments=MD)
    grid_sum = lax.map(owner_forward, owners).reshape(devices * MD, L)
    node_in = jnp.concatenate([mesh_lat, grid_sum.astype(jnp.bfloat16)], axis=1)
    node_pre = jnp.dot(node_in, w_node_in, preferred_element_type=jnp.float32)
    node_upd, node_stash = tail_forward(node_pre, w_node_out, gain_node)
    state_one = mesh_lat.astype(jnp.float32) + node_upd
    state_bf = state_one.astype(jnp.bfloat16)
    proc_terms = jnp.dot(state_bf, w_proc_send, preferred_element_type=jnp.float32).astype(jnp.bfloat16)
    proc_recv_terms = jnp.dot(state_bf, w_proc_recv, preferred_element_type=jnp.float32)
    term_blocks = proc_terms.reshape(devices, MD, L)
    sent = jax.vmap(take_rows)(term_blocks, halo_lists.reshape(devices, 4 * HC)).reshape(N_LAT, N_LON, 4, HC, L)
    zero_block = jnp.zeros((1, N_LON, HC, L), jnp.bfloat16)
    from_below = jnp.concatenate([zero_block, sent[:-1, :, 0]], axis=0)
    from_above = jnp.concatenate([sent[1:, :, 1], zero_block], axis=0)
    from_west = jnp.roll(sent[:, :, 2], 1, axis=1)
    from_east = jnp.roll(sent[:, :, 3], -1, axis=1)
    halo = jnp.stack([from_below, from_above, from_west, from_east], axis=2).reshape(devices, 4 * HC, L)
    table_width = MD + 4 * HC
    sender_table = jnp.concatenate([term_blocks, halo], axis=1).reshape(devices * table_width, L)
    send_glob = (proc_send + (owners * table_width)[:, None]).reshape(-1)
    recv_glob = (proc_recv + (owners * MD)[:, None]).reshape(-1)
    proc_pre = jnp.take(sender_table, send_glob, axis=0).astype(jnp.float32) + jnp.take(proc_recv_terms, recv_glob, axis=0)
    proc_msg, proc_stash = tail_forward(proc_pre, w_proc_out, gain_proc)
    proc_sum = jax.ops.segment_sum(proc_msg, recv_glob, num_segments=devices * MD)
    upd_in = jnp.concatenate([state_bf, proc_sum.astype(jnp.bfloat16)], axis=1)
    upd_pre = jnp.dot(upd_in, w_upd_in, preferred_element_type=jnp.float32)
    upd_out, upd_stash = tail_forward(upd_pre, w_upd_out, gain_upd)
    mesh_out = state_one + upd_out
    grad_top = cotangent.astype(jnp.float32)
    grad_upd_pre, unused_upd = tail_backward(upd_pre, upd_stash, grad_top, w_upd_out, gain_upd)
    grad_upd_in = outer_cols(grad_upd_pre.astype(jnp.bfloat16), w_upd_in)
    grad_state = grad_top + grad_upd_in[:, :L]
    grad_proc_msg = jnp.take(grad_upd_in[:, L:], recv_glob, axis=0)
    grad_proc_pre, grad_proc_out = tail_backward(proc_pre, proc_stash, grad_proc_msg, w_proc_out, gain_proc)
    grad_table = jax.ops.segment_sum(grad_proc_pre, send_glob, num_segments=devices * table_width).reshape(devices, table_width, L)
    grad_recv2 = jax.ops.segment_sum(grad_proc_pre, recv_glob, num_segments=devices * MD)
    grad_halo = grad_table[:, MD:].astype(jnp.bfloat16).reshape(N_LAT, N_LON, 4, HC, L)
    back_below = jnp.concatenate([grad_halo[1:, :, 0], zero_block], axis=0)
    back_above = jnp.concatenate([zero_block, grad_halo[:-1, :, 1]], axis=0)
    back_west = jnp.roll(grad_halo[:, :, 2], -1, axis=1)
    back_east = jnp.roll(grad_halo[:, :, 3], 1, axis=1)
    returned = jnp.stack([back_below, back_above, back_west, back_east], axis=2).reshape(devices * 4 * HC, L).astype(jnp.float32)
    list_glob = (halo_lists.reshape(devices, 4 * HC) + (owners * MD)[:, None]).reshape(-1)
    grad_terms = grad_table[:, :MD].reshape(devices * MD, L) + jax.ops.segment_sum(returned, list_glob, num_segments=devices * MD)
    grad_terms_bf = grad_terms.astype(jnp.bfloat16)
    grad_recv2_bf = grad_recv2.astype(jnp.bfloat16)
    grad_proc_send = inner_rows(state_bf, grad_terms_bf)
    grad_proc_recv = inner_rows(state_bf, grad_recv2_bf)
    grad_state = grad_state + outer_cols(grad_terms_bf, w_proc_send) + outer_cols(grad_recv2_bf, w_proc_recv)
    grad_node_pre, unused_node = tail_backward(node_pre, node_stash, grad_state, w_node_out, gain_node)
    grad_grid_sum = outer_cols(grad_node_pre.astype(jnp.bfloat16), w_node_in[L:])
    grad_blocks = grad_grid_sum.reshape(devices, MD, L)

    def owner_back(carry, owner_dev):
        grad_acc, out_acc, recv_acc = carry
        preact, recv_idx, recv_ok, sources, sender_idx, sender_ok = owner_pre(owner_dev)
        unused_msg, stash = tail_forward(preact, w_grid_out, gain_grid)
        grad_message = jnp.take(grad_blocks[owner_dev], recv_idx, axis=0) * recv_ok[:, None]
        grad_pre, weight_grad = tail_backward(preact, stash, grad_message, w_grid_out, gain_grid)
        grad_recv = jax.ops.segment_sum(grad_pre, recv_idx, num_segments=MD)
        recv_weight = inner_rows(mesh_blocks[owner_dev], grad_recv.astype(jnp.bfloat16))
        rounded = lax.optimization_barrier(grad_pre.astype(jnp.bfloat16)).astype(jnp.float32).reshape(9, CAP, L)
        rounded = jnp.where(sender_ok[:, :, None], rounded, 0.0)
        grad_acc = grad_acc.at[jnp.broadcast_to(sources[:, None], sender_idx.shape), sender_idx].add(rounded)
        return ((grad_acc, out_acc + weight_grad, recv_acc + recv_weight), None)
    start = (jnp.zeros((devices, GD, L), jnp.float32), jnp.zeros((L, L), jnp.float32), jnp.zeros((L, L), jnp.float32))
    finals, unused_scan = lax.scan(owner_back, start, owners)
    grad_grid_terms, grad_grid_out, grad_grid_recv = finals
    grad_terms_grid = grad_grid_terms.reshape(devices * GD, L).astype(jnp.bfloat16)
    grad_grid_send = inner_rows(grid_lat, grad_terms_grid)
    grid_grad = outer_cols(grad_terms_grid, w_grid_send)
    return (mesh_out, grid_grad, grad_grid_send, grad_grid_recv, grad_grid_out, grad_proc_send, grad_proc_recv, grad_proc_out)
```

```python
import jax
import jax.numpy as jnp
from jax import lax
from jax.experimental import pallas as pl
from jax.experimental.pallas import tpu as pltpu
from jax.sharding import PartitionSpec as P

EPSILON = 1e-05
product_precision = lax.Precision.DEFAULT


def passed_along(value, axis, steps):
    count = lax.axis_size(axis)
    first, last = (max(0, -steps), min(count, count - steps))
    return lax.ppermute(value, axis, [(source, source + steps) for source in range(first, last)])


def passed_along_2(block, axis, distance):
    devices = range(lax.axis_size(axis))
    route = [((i - distance) % len(devices), i) for i in devices]
    return lax.ppermute(block, axis, route)


def inner_rows(matrix_one, matrix_two, precision=None):
    return lax.dot_general(
        matrix_one,
        matrix_two,
        (((0,), (0,)), ((), ())),
        precision=precision,
        preferred_element_type=jnp.float32,
    )


def outer_cols(matrix_one, matrix_two):
    return lax.dot_general(
        matrix_one, matrix_two, (((1,), (1,)), ((), ())), preferred_element_type=jnp.float32
    )


def tail_forward(preact, weight_out, gain_vec):
    sigmoid_act = jax.nn.sigmoid(preact)
    hidden = (preact * sigmoid_act).astype(jnp.bfloat16)
    mixed_out = jnp.dot(hidden, weight_out, preferred_element_type=jnp.float32)
    centre = mixed_out - jnp.mean(mixed_out, axis=-1, keepdims=True)
    inv_std = lax.rsqrt(jnp.mean(centre * centre, axis=-1, keepdims=True) + EPSILON)
    normed = centre * inv_std
    return (normed * gain_vec, (sigmoid_act, hidden, normed, inv_std))


def tail_backward(preact, stash, grad_out, weight_out, gain_vec):
    sigmoid_act, hidden, normed, inv_std = stash
    upstream = grad_out * gain_vec
    grad_mixed = inv_std * (
        upstream
        - jnp.mean(upstream, axis=-1, keepdims=True)
        - normed * jnp.mean(upstream * normed, axis=-1, keepdims=True)
    )
    grad_mixed = grad_mixed.astype(jnp.bfloat16)
    weight_grad = inner_rows(hidden, grad_mixed)
    grad_hidden = outer_cols(grad_mixed, weight_out)
    slope = sigmoid_act + preact * sigmoid_act * (1.0 - sigmoid_act)
    return (grad_hidden * slope, weight_grad)


def tiles_lat(block, shift_by):
    return passed_along(block, "lat", shift_by)


def tiles_lon(block, shift_by):
    return passed_along_2(block, "lon", shift_by)


def grads_lat(block, shift_by):
    return passed_along(block, "lat", shift_by)


def grads_lon(block, shift_by):
    return passed_along_2(block, "lon", shift_by)


def send_terms(slots):
    blocks = slots.reshape((3, 3) + slots.shape[1:])
    rows = jnp.stack([tiles_lat(blocks[0], -1), blocks[1], tiles_lat(blocks[2], 1)], axis=0)
    moved = jnp.stack([tiles_lon(rows[:, 0], -1), rows[:, 1], tiles_lon(rows[:, 2], 1)], axis=1)
    return moved.reshape(slots.shape)


def send_grads(slots):
    blocks = slots.reshape((3, 3) + slots.shape[1:])
    cols = jnp.stack(
        [grads_lon(blocks[:, 0], 1), blocks[:, 1], grads_lon(blocks[:, 2], -1)], axis=1
    )
    moved = jnp.stack([grads_lat(cols[0], 1), cols[1], grads_lat(cols[2], -1)], axis=0)
    return moved.reshape(slots.shape)


def along_lat(block, shift_by):
    return passed_along(block, "lat", shift_by)


def along_lon(block, shift_by):
    return passed_along_2(block, "lon", shift_by)


def return_lat(block, shift_by):
    return passed_along(block, "lat", shift_by)


def return_lon(block, shift_by):
    return passed_along_2(block, "lon", shift_by)


MESH = pl.DeviceIdType.MESH
ORDERS = ((0, 1, 2), (1, 2, 0), (2, 0, 1))


def coordinates():
    lon = lax.axis_index("lon")
    return (lax.axis_index("lat"), lon // 8, lax.rem(lon // 2, 4), lax.rem(lon, 2))


def device(z, x, y, c):
    return (z, (x * 4 + y) * 2 + c)


def ring_peer(me, dim, step):
    spot = list(me)
    spot[dim] = lax.rem(me[dim] + step, 4)
    return device(*spot)


def core_peer(me):
    return device(me[0], me[1], me[2], 1 - me[3])


def greet(peers):
    barrier = pltpu.get_barrier_semaphore()
    for peer in peers:
        pl.semaphore_signal(barrier, inc=1, device_id=peer, device_id_type=MESH)
    pl.semaphore_wait(barrier, len(peers))


class Reduction:
    def __init__(self, me, order, source, bufs, send, recv):
        self.me, self.order, self.source = me, ORDERS[order], source
        self.s0, self.r0, self.s1, self.r1, self.s2, self.r2, self.s3, self.r3, self.full = bufs
        self.send, self.recv = send, recv
        self.spot = [me[d] for d in self.order]
        self.copies = {}

    def start(self, slot, src, dst, peer):
        copy = pltpu.make_async_remote_copy(
            src_ref=src, dst_ref=dst, send_sem=self.send.at[slot], recv_sem=self.recv.at[slot],
            device_id=peer, device_id_type=MESH,
        )
        copy.start()
        self.copies[slot] = copy

    def begin(self):
        other = pl.multiple_of((1 - self.me[3]) * 256, 256)
        self.s0[...] = self.source[pl.ds(other, 256), :].astype(jnp.bfloat16)
        self.start(0, self.s0, self.r0, core_peer(self.me))

    def scatter(self, level):
        own = self.spot[level]
        if level == 0:
            self.copies[0].wait_recv()
            mine = pl.multiple_of(self.me[3] * 256, 256)
            total = self.source[pl.ds(mine, 256), :] + self.r0[...].astype(jnp.float32)
            self.s1[...] = total.astype(jnp.bfloat16).reshape(4, 64, 512)
            sends, lands, base = self.s1, self.r1, 1
        elif level == 1:
            self.arrive(1)
            total = self.s1[self.spot[0]].astype(jnp.float32)
            for k in range(3):
                total = total + self.r1[k].astype(jnp.float32)
            self.s2[...] = total.astype(jnp.bfloat16).reshape(4, 16, 512)
            sends, lands, base = self.s2, self.r2, 4
        else:
            self.arrive(4)
            total = self.s2[self.spot[1]].astype(jnp.float32)
            for k in range(3):
                total = total + self.r2[k].astype(jnp.float32)
            total = total.astype(jnp.bfloat16)
            for j in range(4):
                self.s3[j] = total[:, j * 128 : (j + 1) * 128]
            sends, lands, base = self.s3, self.r3, 7
        for step in (1, 3, 2):
            goal = lax.rem(own + step, 4)
            self.start(base + step - 1, sends.at[goal], lands.at[step - 1], ring_peer(self.me, self.order[level], step))

    def arrive(self, base):
        for k in range(3):
            self.copies[base + k].wait_recv()

    def place(self, level):
        spots = (self.me[3], *self.spot)
        return self.full.at[spots[: level + 1]]

    def gather(self, level):
        if level == 3:
            self.arrive(7)
            total = self.s3[self.spot[2]].astype(jnp.float32)
            for k in range(3):
                total = total + self.r3[k].astype(jnp.float32)
            a, b, c = self.spot
            self.full[self.me[3], a, b, c] = total.astype(jnp.bfloat16)
        else:
            self.arrive(10 + 3 * (2 - level))
        base = 10 + 3 * (3 - level)
        block = self.place(level)
        if level == 0:
            self.start(19, block, block, core_peer(self.me))
        else:
            for step in (1, 3, 2):
                self.start(base + step - 1, block, block, ring_peer(self.me, self.order[level - 1], step))

    def finish(self):
        self.copies[19].wait_recv()
        for copy in self.copies.values():
            copy.wait_send()


def reduction_scratch(count):
    shapes = ((256, 512), (256, 512), (4, 64, 512), (3, 64, 512), (4, 16, 512), (3, 16, 512), (4, 16, 128), (3, 16, 128))
    return [pltpu.VMEM((count,) + s, jnp.bfloat16) for s in shapes]


def reduce_kernel(*refs):
    grads, full = refs[:6], refs[6]
    bufs, send, recv = refs[7:15], refs[15], refs[16]
    me = coordinates()
    greet([core_peer(me)] + [ring_peer(me, d, s) for d in range(3) for s in (1, 2, 3)])
    parts = [
        Reduction(me, g % 3, grads[g], [b.at[g] for b in bufs] + [full.at[g]], send.at[g], recv.at[g])
        for g in range(6)
    ]
    for part in parts:
        part.begin()
    for level in range(3):
        for part in parts:
            part.scatter(level)
    for level in (3, 2, 1, 0):
        for part in parts:
            part.gather(level)
    for part in parts:
        part.finish()


def spread_kernel(full, *outs):
    for g, out in enumerate(outs):
        def rows(i, carry):
            h, rest = i // 16, lax.rem(i, 16)
            a, b = rest // 4, lax.rem(rest, 4)
            for c in range(4):
                out[pl.ds(pl.multiple_of(i * 16, 16), 16), c * 128 : (c + 1) * 128] = full[g, h, a, b, c].astype(jnp.float32)
            return carry
        lax.fori_loop(0, 32, rows, 0)


def reduced(grads):
    vmem = pl.BlockSpec(memory_space=pltpu.VMEM)
    full = pl.pallas_call(
        reduce_kernel,
        out_shape=jax.ShapeDtypeStruct((6, 2, 4, 4, 4, 16, 128), jnp.bfloat16),
        in_specs=[vmem] * 6,
        out_specs=vmem,
        scratch_shapes=reduction_scratch(6) + [pltpu.SemaphoreType.DMA((6, 20)), pltpu.SemaphoreType.DMA((6, 20))],
        compiler_params=pltpu.CompilerParams(collective_id=0, has_side_effects=True, vmem_limit_bytes=60 << 20),
        name="reduce",
    )(*grads)
    return pl.pallas_call(
        spread_kernel,
        out_shape=[jax.ShapeDtypeStruct((512, 512), jnp.float32)] * 6,
        in_specs=[vmem],
        out_specs=[vmem] * 6,
        name="spread",
    )(full)


def local(
    grid_lat,
    mesh_lat,
    g2m_send,
    g2m_recv,
    g2m_feat,
    halo_lists,
    proc_send,
    proc_recv,
    cotangent,
    w_grid_send,
    w_grid_recv,
    w_grid_feat,
    w_grid_out,
    gain_grid,
    w_node_in,
    w_node_out,
    gain_node,
    w_proc_send,
    w_proc_recv,
    w_proc_out,
    gain_proc,
    w_upd_in,
    w_upd_out,
    gain_upd,
):
    width = mesh_lat.shape[1]
    grid_count = grid_lat.shape[0]
    mesh_count = mesh_lat.shape[0]
    senders = g2m_send[0]
    offset_count, capacity = senders.shape
    sender_ok = senders >= 0
    sender_idx = jnp.maximum(senders, 0).reshape(-1)
    grid_terms = jnp.dot(grid_lat, w_grid_send, preferred_element_type=jnp.float32)
    picked = jnp.take(grid_terms, sender_idx, axis=0).reshape(offset_count, capacity, width)
    slots = jnp.where(sender_ok[:, :, None], picked, 0.0).astype(jnp.bfloat16)
    arrived = send_terms(slots).reshape(offset_count * capacity, width)
    receivers = g2m_recv[0].reshape(-1)
    recv_ok = (receivers >= 0).astype(jnp.float32)
    recv_idx = jnp.maximum(receivers, 0)
    mesh_ids = jnp.arange(mesh_count, dtype=jnp.int32)
    onehot_grid = (receivers[:, None] == mesh_ids[None, :]).astype(jnp.float32)
    recv_terms = jnp.dot(mesh_lat, w_grid_recv, preferred_element_type=jnp.float32)
    edge_terms = inner_rows(g2m_feat[0], w_grid_feat)
    grid_pre = arrived.astype(jnp.float32) + jnp.take(recv_terms, recv_idx, axis=0) + edge_terms
    message, grid_stash = tail_forward(grid_pre, w_grid_out, gain_grid)
    message = message * recv_ok[:, None]
    grid_sum = inner_rows(onehot_grid, message, product_precision)
    node_in = jnp.concatenate([mesh_lat, grid_sum.astype(jnp.bfloat16)], axis=1)
    node_pre = jnp.dot(node_in, w_node_in, preferred_element_type=jnp.float32)
    node_upd, node_stash = tail_forward(node_pre, w_node_out, gain_node)
    state_one = mesh_lat.astype(jnp.float32) + node_upd
    state_bf = state_one.astype(jnp.bfloat16)
    proc_terms = jnp.dot(state_bf, w_proc_send, preferred_element_type=jnp.float32).astype(
        jnp.bfloat16
    )
    proc_recv_terms = jnp.dot(state_bf, w_proc_recv, preferred_element_type=jnp.float32)
    halo_rows = halo_lists[0]
    halo_count = halo_rows.shape[1]
    outgoing = jnp.take(proc_terms, halo_rows.reshape(-1), axis=0).reshape(4, halo_count, width)
    incoming = [
        along_lat(outgoing[0], 1),
        along_lat(outgoing[1], -1),
        along_lon(outgoing[2], 1),
        along_lon(outgoing[3], -1),
    ]
    sender_table = jnp.concatenate([proc_terms] + incoming, axis=0)
    edge_from = proc_send[0]
    edge_to = proc_recv[0]
    table_ids = jnp.arange(sender_table.shape[0], dtype=jnp.int32)
    onehot_from = (edge_from[:, None] == table_ids[None, :]).astype(jnp.float32)
    onehot_to = (edge_to[:, None] == mesh_ids[None, :]).astype(jnp.float32)
    proc_pre = jnp.take(sender_table, edge_from, axis=0).astype(jnp.float32) + jnp.take(
        proc_recv_terms, edge_to, axis=0
    )
    proc_msg, proc_stash = tail_forward(proc_pre, w_proc_out, gain_proc)
    proc_sum = inner_rows(onehot_to, proc_msg, product_precision)
    upd_in = jnp.concatenate([state_bf, proc_sum.astype(jnp.bfloat16)], axis=1)
    upd_pre = jnp.dot(upd_in, w_upd_in, preferred_element_type=jnp.float32)
    upd_out, upd_stash = tail_forward(upd_pre, w_upd_out, gain_upd)
    mesh_out = state_one + upd_out
    grad_top = cotangent.astype(jnp.float32)
    grad_upd_pre, unused_upd = tail_backward(upd_pre, upd_stash, grad_top, w_upd_out, gain_upd)
    grad_upd_in = outer_cols(grad_upd_pre.astype(jnp.bfloat16), w_upd_in)
    grad_state = grad_top + grad_upd_in[:, :width]
    grad_proc_msg = jnp.dot(onehot_to, grad_upd_in[:, width:])
    grad_proc_pre, grad_proc_out = tail_backward(
        proc_pre, proc_stash, grad_proc_msg, w_proc_out, gain_proc
    )
    grad_table = inner_rows(onehot_from, grad_proc_pre, product_precision)
    grad_recv2 = inner_rows(onehot_to, grad_proc_pre, product_precision)
    grad_halo = grad_table[mesh_count:].astype(jnp.bfloat16).reshape(4, halo_count, width)
    returned = jnp.stack(
        [
            return_lat(grad_halo[0], -1),
            return_lat(grad_halo[1], 1),
            return_lon(grad_halo[2], -1),
            return_lon(grad_halo[3], 1),
        ],
        axis=0,
    )
    returned = returned.reshape(4 * halo_count, width).astype(jnp.float32)
    onehot_halo = (halo_rows.reshape(-1)[:, None] == mesh_ids[None, :]).astype(jnp.float32)
    grad_terms = grad_table[:mesh_count] + inner_rows(onehot_halo, returned, product_precision)
    grad_terms_bf = grad_terms.astype(jnp.bfloat16)
    grad_recv2_bf = grad_recv2.astype(jnp.bfloat16)
    grad_proc_send = inner_rows(state_bf, grad_terms_bf)
    grad_proc_recv = inner_rows(state_bf, grad_recv2_bf)
    grad_state = (
        grad_state + outer_cols(grad_terms_bf, w_proc_send) + outer_cols(grad_recv2_bf, w_proc_recv)
    )
    grad_node_pre, unused_node = tail_backward(
        node_pre, node_stash, grad_state, w_node_out, gain_node
    )
    grad_grid_sum = outer_cols(grad_node_pre.astype(jnp.bfloat16), w_node_in[width:])
    grad_message = jnp.dot(onehot_grid, grad_grid_sum)
    grad_grid_pre, grad_grid_out = tail_backward(
        grid_pre, grid_stash, grad_message, w_grid_out, gain_grid
    )
    grad_recv_terms = inner_rows(onehot_grid, grad_grid_pre, product_precision)
    grad_grid_recv = inner_rows(mesh_lat, grad_recv_terms.astype(jnp.bfloat16))
    slot_grads = grad_grid_pre.astype(jnp.bfloat16).reshape(offset_count, capacity, width)
    back_slots = send_grads(slot_grads).astype(jnp.float32)
    back_slots = jnp.where(sender_ok[:, :, None], back_slots, 0.0).reshape(
        offset_count * capacity, width
    )
    grad_grid_terms = jax.ops.segment_sum(back_slots, sender_idx, num_segments=grid_count)
    grad_grid_bf = grad_grid_terms.astype(jnp.bfloat16)
    grad_grid_send = inner_rows(grid_lat, grad_grid_bf)
    grid_grad = outer_cols(grad_grid_bf, w_grid_send)
    summed = reduced(
        (
            grad_grid_send,
            grad_grid_recv,
            grad_grid_out,
            grad_proc_send,
            grad_proc_recv,
            grad_proc_out,
        )
    )
    return (mesh_out, grid_grad) + tuple(summed)


def solution(mesh):
    placed = (
        P(("lat", "lon"), None),
        P(("lat", "lon"), None),
        P(("lat", "lon"), None, None),
        P(("lat", "lon"), None, None),
        P(("lat", "lon"), None, None),
        P(("lat", "lon"), None, None),
        P(("lat", "lon"), None),
        P(("lat", "lon"), None),
        P(("lat", "lon"), None),
        P(),
        P(),
        P(),
        P(),
        P(),
        P(),
        P(),
        P(),
        P(),
        P(),
        P(),
        P(),
        P(),
        P(),
        P(),
    )
    return jax.shard_map(
        local,
        mesh=mesh,
        in_specs=placed,
        out_specs=(P(("lat", "lon"), None), P(("lat", "lon"), None), P(), P(), P(), P(), P(), P()),
        check_vma=False,
    )
```

```python
import functools

import jax
import jax.numpy as jnp
from jax import lax
from jax.experimental import pallas as pl
from jax.experimental.pallas import tpu as pltpu
from jax.sharding import PartitionSpec as P

EPSILON = 1e-05
MESH = pl.DeviceIdType.MESH
ORDERS = ((0, 1, 2), (1, 2, 0), (2, 0, 1))
BF = jnp.bfloat16
F32 = jnp.float32


def mm(a, b):
    return jnp.dot(a, b, preferred_element_type=F32)


def mm_t(a, b):
    return lax.dot_general(a, b, (((0,), (0,)), ((), ())), preferred_element_type=F32)


def mm_nt(a, b):
    return lax.dot_general(a, b, (((1,), (1,)), ((), ())), preferred_element_type=F32)


def tail_forward(pre, weight):
    sig = jax.nn.sigmoid(pre)
    hid = (pre * sig).astype(BF)
    z = mm(hid, weight)
    centre = z - jnp.mean(z, axis=-1, keepdims=True)
    inv = lax.rsqrt(jnp.mean(centre * centre, axis=-1, keepdims=True) + EPSILON)
    return hid, centre * inv, inv, sig + pre * sig * (1.0 - sig)


def tail_backward(grad, gain, zhat, inv, slope, weight):
    u = grad * gain
    m1 = jnp.mean(u, axis=-1, keepdims=True)
    m2 = jnp.mean(u * zhat, axis=-1, keepdims=True)
    dz = (inv * (u - m1 - zhat * m2)).astype(BF)
    return dz, mm_nt(dz, weight) * slope


def coordinates():
    lon = lax.axis_index("lon")
    return (lax.axis_index("lat"), lon // 8, lax.rem(lon // 2, 4), lax.rem(lon, 2))


def device(z, x, y, c):
    return (z, (x * 4 + y) * 2 + c)


def ring_peer(me, dim, step):
    spot = list(me)
    spot[dim] = lax.rem(me[dim] + step, 4)
    return device(*spot)


def core_peer(me):
    return device(me[0], me[1], me[2], 1 - me[3])


def tile_peer(dlat, dlon):
    return (lax.rem(lax.axis_index("lat") + dlat + 4, 4), lax.rem(lax.axis_index("lon") + dlon + 32, 32))


def offset_peer(k, sign):
    return tile_peer(sign * (k // 3 - 1), sign * (lax.rem(k, 3) - 1))


def greet(peers):
    barrier = pltpu.get_barrier_semaphore()
    for peer in peers:
        pl.semaphore_signal(barrier, inc=1, device_id=peer, device_id_type=MESH)
    pl.semaphore_wait(barrier, len(peers))


def push(src, dst, send, recv, peer):
    return pltpu.make_async_remote_copy(
        src_ref=src, dst_ref=dst, send_sem=send, recv_sem=recv, device_id=peer, device_id_type=MESH
    )


class Reduction:
    def __init__(self, order, source, bufs, send, recv):
        self.order, self.source = ORDERS[order], source
        self.s0, self.r0, self.s1, self.r1, self.s2, self.r2, self.s3, self.r3, self.full = bufs
        self.send, self.recv = send, recv

    def copy(self, slot):
        me = coordinates()
        spot = [me[d] for d in self.order]
        if slot == 0:
            src, dst, peer = self.s0, self.r0, core_peer(me)
        elif slot < 10:
            level, step = (slot - 1) // 3, (slot - 1) % 3 + 1
            sends = (self.s1, self.s2, self.s3)[level]
            lands = (self.r1, self.r2, self.r3)[level]
            src, dst = sends.at[lax.rem(spot[level] + step, 4)], lands.at[step - 1]
            peer = ring_peer(me, self.order[level], step)
        else:
            level = 3 - (slot - 10) // 3
            src = dst = self.full.at[(me[3], *spot)[: level + 1]]
            step = (slot - 10) % 3 + 1
            peer = core_peer(me) if level == 0 else ring_peer(me, self.order[level - 1], step)
        return push(src, dst, self.send.at[slot], self.recv.at[slot], peer)

    def arrive(self, base):
        for k in range(3):
            self.copy(base + k).wait_recv()

    def depart(self, base):
        for step in (1, 3, 2):
            self.copy(base + step - 1).start()

    def begin(self):
        other = pl.multiple_of((1 - coordinates()[3]) * 256, 256)
        self.s0[...] = self.source[pl.ds(other, 256), :].astype(BF)
        self.copy(0).start()

    def scatter(self, level):
        me = coordinates()
        spot = [me[d] for d in self.order]
        if level == 0:
            self.copy(0).wait_recv()
            mine = pl.multiple_of(me[3] * 256, 256)
            total = self.source[pl.ds(mine, 256), :] + self.r0[...].astype(F32)
            self.s1[...] = total.astype(BF).reshape(4, 64, 512)
        else:
            self.arrive(3 * level - 2)
            sends, lands = (self.s1, self.s2)[level - 1], (self.r1, self.r2)[level - 1]
            total = sends[spot[level - 1]].astype(F32)
            for k in range(3):
                total = total + lands[k].astype(F32)
            total = total.astype(BF)
            if level == 1:
                self.s2[...] = total.reshape(4, 16, 512)
            else:
                for j in range(4):
                    self.s3[j] = total[:, j * 128 : (j + 1) * 128]
        self.depart(3 * level + 1)

    def gather(self, level):
        if level == 3:
            me = coordinates()
            a, b, c = [me[d] for d in self.order]
            self.arrive(7)
            total = self.s3[c].astype(F32)
            for k in range(3):
                total = total + self.r3[k].astype(F32)
            self.full[me[3], a, b, c] = total.astype(BF)
        else:
            self.arrive(10 + 3 * (2 - level))
        if level == 0:
            self.copy(19).start()
        else:
            self.depart(10 + 3 * (3 - level))

    def finish(self):
        self.copy(19).wait_recv()
        for slot in range(20):
            self.copy(slot).wait_send()


def reduction_scratch(count):
    shapes = ((256, 512), (256, 512), (4, 64, 512), (3, 64, 512), (4, 16, 512), (3, 16, 512), (4, 16, 128), (3, 16, 128))
    return [pltpu.VMEM((count,) + s, BF) for s in shapes]


OWN = 4
INPUTS = 25


def ahead(i):
    return lax.rem(i + 5, 9)


def main_kernel(*refs):
    (grid_lat, mesh_lat, send_rows, aux, halo_row, from_row, to_row, cot, w_grid_send, w_grid_recv, w_feat, w_grid_out,
     gain_grid, w_node_in, w_node_out, gain_node, w_proc_send, w_proc_recv, w_proc_out, gain_proc, w_upd_in, w_upd_out,
     gain_upd) = refs[:23]
    full, d_terms, mesh_out = refs[23:26]
    red = refs[26:34]
    (red_send, red_recv, grads, mesh_in, aux_in, part_out, part_in, dsum_out, dsum_in, halo_out, table, back_out, back_in,
     terms, slots, recv_hl, hid_s, zhat_s, slope_s, inv_s, dpre_s, drecv_s, cols, ex_send, ex_recv) = refs[34:]
    me = coordinates()
    greet([offset_peer(k, 1) for k in range(9) if k != OWN] + [core_peer(me)] + [ring_peer(me, d, s) for d in range(3) for s in (1, 2, 3)])

    def mesh_copy(k):
        return push(mesh_lat, mesh_in.at[k], ex_send.at[0, k], ex_recv.at[0, k], offset_peer(k, -1))

    def aux_copy(k):
        return push(aux.at[k], aux_in.at[k], ex_send.at[1, k], ex_recv.at[1, k], offset_peer(k, -1))

    def part_copy(k):
        return push(part_out.at[k], part_in.at[k], ex_send.at[2, k], ex_recv.at[2, k], offset_peer(k, 1))

    def dsum_copy(k):
        return push(dsum_out, dsum_in.at[k], ex_send.at[3, k], ex_recv.at[3, k], offset_peer(k, -1))

    ways = ((1, 0), (-1, 0), (0, 1), (0, -1))

    def halo_copy(j):
        return push(halo_out.at[pl.ds(16 * j, 16)], table.at[pl.ds(64 + 16 * j, 16)], ex_send.at[4, j], ex_recv.at[4, j], tile_peer(*ways[j]))

    def back_copy(j):
        dlat, dlon = ways[j]
        return push(back_out.at[pl.ds(16 * j, 16)], back_in.at[pl.ds(16 * j, 16)], ex_send.at[5, j], ex_recv.at[5, j], tile_peer(-dlat, -dlon))

    def each(copy):
        for k in (0, 2, 6, 8, 1, 7, 3, 5):
            copy(k).start()

    each(aux_copy)
    each(mesh_copy)
    mesh_in[OWN] = mesh_lat[...]
    aux_in[OWN] = aux[OWN]

    def terms_body(i, carry):
        rows = pl.ds(pl.multiple_of(i * 256, 256), 256)
        terms[rows, :] = mm(grid_lat[rows, :], w_grid_send[...]).astype(BF)
        return carry

    lax.fori_loop(0, 4, terms_body, 0)
    padded = jnp.concatenate([send_rows[...].astype(F32), jnp.zeros((7, 256), F32)], axis=0)
    cols[...] = jnp.transpose(padded)

    def slots_body(k, carry):
        lane = lax.broadcasted_iota(jnp.int32, (256, 16), 1)
        col = jnp.sum(jnp.where(lane == k, cols[...], 0.0), axis=1, keepdims=True).astype(jnp.int32)
        pick = (col == lax.broadcasted_iota(jnp.int32, (256, 1024), 1)).astype(F32).astype(BF)
        slots[k] = mm(pick, terms[...]).astype(BF)
        return carry

    lax.fori_loop(0, 9, slots_body, 0)
    for k in range(9):
        if k != OWN:
            mesh_copy(k).wait_recv()
            aux_copy(k).wait_recv()

    def recv_body(k, carry):
        full_terms = mm(mesh_in[k], w_grid_recv[...])
        high = full_terms.astype(BF)
        recv_hl[k, :64, :] = high
        recv_hl[k, 64:, :] = (full_terms - high.astype(F32)).astype(BF)
        return carry

    lax.fori_loop(0, 9, recv_body, 0)

    def receivers(k):
        index = aux_in[k].astype(F32)[4:5, :].astype(jnp.int32)
        return (index == lax.broadcasted_iota(jnp.int32, (64, 256), 0)).astype(F32).astype(BF)

    def forward_body(i, carry):
        k = ahead(i)
        rec = receivers(k)
        left = jnp.concatenate([rec, rec, aux_in[k]], axis=0)
        right = jnp.concatenate([recv_hl[k], w_feat[...]], axis=0)
        pre = slots[k].astype(F32) + mm_t(left, right)
        hid, zhat, inv, slope = tail_forward(pre, w_grid_out[...])
        hid_s[k], zhat_s[k], slope_s[k] = hid, zhat.astype(BF), slope.astype(BF)
        inv_s[k] = inv
        part_out[k] = (mm(rec, zhat.astype(BF)) * gain_grid[...]).astype(BF)

        @pl.when(k != OWN)
        def _():
            part_copy(k).start()

        return carry

    lax.fori_loop(0, 9, forward_body, 0)

    grid_sum = part_out[OWN].astype(F32)
    for k in range(9):
        if k != OWN:
            part_copy(k).wait_recv()
            grid_sum = grid_sum + part_in[k].astype(F32)
    node_pre = mm(mesh_lat[...], w_node_in[:512, :]) + mm(grid_sum.astype(BF), w_node_in[512:, :])
    node_hid, node_zhat, node_inv, node_slope = tail_forward(node_pre, w_node_out[...])
    state = mesh_lat[...].astype(F32) + node_zhat * gain_node[...]
    state_bf = state.astype(BF)
    own_terms = mm(state_bf, w_proc_send[...]).astype(BF)
    lists = (halo_row[...] == lax.broadcasted_iota(jnp.int32, (64, 64), 0)).astype(F32).astype(BF)
    halo_out[...] = mm_t(lists, own_terms).astype(BF)
    for j in range(4):
        halo_copy(j).start()
    table[:64, :] = own_terms
    p_recv = mm(state_bf, w_proc_recv[...])
    p_high = p_recv.astype(BF)
    p_low = (p_recv - p_high.astype(F32)).astype(BF)
    pick_from = (from_row[...] == lax.broadcasted_iota(jnp.int32, (128, 512), 0)).astype(F32).astype(BF)
    pick_to = (to_row[...] == lax.broadcasted_iota(jnp.int32, (64, 512), 0)).astype(F32).astype(BF)
    for j in range(4):
        halo_copy(j).wait_recv()
    left = jnp.concatenate([pick_from, pick_to, pick_to], axis=0)
    right = jnp.concatenate([table[...], p_high, p_low], axis=0)
    proc_pre = mm_t(left, right)
    p_hid, p_zhat, p_inv, p_slope = tail_forward(proc_pre, w_proc_out[...])
    proc_sum = mm(pick_to, p_zhat.astype(BF)) * gain_proc[...]
    upd_pre = mm(state_bf, w_upd_in[:512, :]) + mm(proc_sum.astype(BF), w_upd_in[512:, :])
    upd_hid, upd_zhat, upd_inv, upd_slope = tail_forward(upd_pre, w_upd_out[...])
    mesh_out[...] = state + upd_zhat * gain_upd[...]
    top = cot[...].astype(F32)
    d_upd = tail_backward(top, gain_upd[...], upd_zhat, upd_inv, upd_slope, w_upd_out[...])[1].astype(BF)
    d_sum = mm_nt(d_upd, w_upd_in[512:, :])
    d_state = top + mm_nt(d_upd, w_upd_in[:512, :])
    d_msg = mm_t(pick_to, d_sum.astype(BF))
    dz, d_pre = tail_backward(d_msg, gain_proc[...], p_zhat, p_inv, p_slope, w_proc_out[...])
    d_pre = d_pre.astype(BF)
    d_table = mm(pick_from, d_pre)
    back_out[...] = d_table[64:, :].astype(BF)
    for j in range(4):
        back_copy(j).start()
    d_recv2 = mm(pick_to, d_pre).astype(BF)
    d_state = d_state + mm_nt(d_recv2, w_proc_recv[...])
    grads[3] = mm_t(p_hid, dz)
    grads[4] = mm_t(state_bf, d_recv2)
    for j in range(4):
        back_copy(j).wait_recv()
    d_own = (d_table[:64, :] + mm(lists, back_in[...])).astype(BF)
    d_state = d_state + mm_nt(d_own, w_proc_send[...])
    d_node = tail_backward(d_state, gain_node[...], node_zhat, node_inv, node_slope, w_node_out[...])[1].astype(BF)
    dsum_out[...] = mm_nt(d_node, w_node_in[512:, :]).astype(BF)
    each(dsum_copy)
    dsum_in[OWN] = dsum_out[...]
    grads[5] = mm_t(state_bf, d_own)
    parts = [
        Reduction(g % 3, grads.at[g], [b.at[g] for b in red] + [full.at[g]], red_send.at[g], red_recv.at[g])
        for g in range(6)
    ]
    early = parts[3:]
    for part in early:
        part.begin()

    grads[0] = jnp.zeros((512, 512), F32)
    grads[2] = jnp.zeros((512, 512), F32)
    stages = [functools.partial(Reduction.scatter, level=v) for v in range(3)] + [
        functools.partial(Reduction.gather, level=v) for v in (3, 2, 1, 0)
    ]

    def backward_body(i, carry):
        k = lax.rem(i + OWN, 9)

        @pl.when(k != OWN)
        def _():
            dsum_copy(k).wait_recv()

        for at, stage in enumerate(stages):

            @pl.when(i == at + 1)
            def _(stage=stage):
                for part in early:
                    stage(part)

        rec = receivers(k)
        grad = mm_t(rec, dsum_in[k])
        zhat = zhat_s[k].astype(F32)
        dz, dpre = tail_backward(grad, gain_grid[...], zhat, inv_s[k], slope_s[k].astype(F32), w_grid_out[...])
        grads[2] += mm_t(hid_s[k], dz)
        dpre = dpre.astype(BF)
        dpre_s[k] = dpre
        drecv_s[k] = mm(rec, dpre).astype(BF)
        return carry

    lax.fori_loop(0, 9, backward_body, 0)
    late = (parts[2], parts[1])
    parts[2].begin()
    grads[1] = mm_t(mesh_in[...].reshape(576, 512), drecv_s[...].reshape(576, 512))
    parts[1].begin()
    every = jnp.concatenate([send_rows[k : k + 1, :] for k in range(9)], axis=1)

    def terms_back(i, carry):
        rows = pl.ds(pl.multiple_of(i * 256, 256), 256)
        ids = lax.broadcasted_iota(jnp.int32, (256, 2304), 0) + i * 256
        put = (every == ids).astype(F32).astype(BF)
        d = mm(put, dpre_s[...].reshape(2304, 512)).astype(BF)
        d_terms[rows, :] = d
        grads[0] += mm_t(grid_lat[rows, :], d)
        return carry

    lax.fori_loop(0, 2, terms_back, 0)
    for part in late:
        stages[0](part)
    lax.fori_loop(2, 4, terms_back, 0)
    parts[0].begin()
    for at in range(1, 7):
        for part in late:
            stages[at](part)
        stages[at - 1](parts[0])
    stages[6](parts[0])
    for part in early:
        part.finish()
    for part in late:
        part.finish()
    parts[0].finish()
    for k in range(9):
        if k != OWN:
            for copy in (mesh_copy, aux_copy, part_copy, dsum_copy):
                copy(k).wait_send()
    for j in range(4):
        halo_copy(j).wait_send()
        back_copy(j).wait_send()


def finish_kernel(full, d_terms, w_grid_send, mesh_in, *outs):
    for g in range(6):
        for b in range(4):
            for c in range(4):
                outs[g][b * 16 : (b + 1) * 16, c * 128 : (c + 1) * 128] = full[g, 0, 0, b, c].astype(F32)
    outs[6][...] = mm_nt(d_terms[...], w_grid_send[...])
    outs[7][...] = mesh_in[...]


def local(
    grid_lat,
    mesh_lat,
    g2m_send,
    g2m_recv,
    g2m_feat,
    halo_lists,
    proc_send,
    proc_recv,
    cotangent,
    w_grid_send,
    w_grid_recv,
    w_grid_feat,
    w_grid_out,
    gain_grid,
    w_node_in,
    w_node_out,
    gain_node,
    w_proc_send,
    w_proc_recv,
    w_proc_out,
    gain_proc,
    w_upd_in,
    w_upd_out,
    gain_upd,
):
    feat = g2m_feat[0].reshape(4, 9, 256).transpose(1, 0, 2)
    recv = g2m_recv[0][:, None, :].astype(BF)
    aux = jnp.concatenate([feat, recv, jnp.zeros((9, 11, 256), BF)], axis=1)
    w_feat = jnp.pad(w_grid_feat, ((0, 12), (0, 0)))
    row = lambda gain: gain.reshape(1, 512)
    vmem = pl.BlockSpec(memory_space=pltpu.VMEM)
    dma = pltpu.SemaphoreType.DMA
    block = lambda *shape: pltpu.VMEM(shape, BF)
    full, d_terms, mesh_new = pl.pallas_call(
        main_kernel,
        out_shape=[
            jax.ShapeDtypeStruct((6, 2, 4, 4, 4, 16, 128), BF),
            jax.ShapeDtypeStruct((1024, 512), BF),
            jax.ShapeDtypeStruct((64, 512), F32),
        ],
        in_specs=[vmem] * 23,
        out_specs=[vmem] * 3,
        scratch_shapes=reduction_scratch(6)
        + [
            dma((6, 20)),
            dma((6, 20)),
            pltpu.VMEM((6, 512, 512), F32),
            block(9, 64, 512),
            block(9, 16, 256),
            block(9, 64, 512),
            block(9, 64, 512),
            block(64, 512),
            block(9, 64, 512),
            block(64, 512),
            block(128, 512),
            block(64, 512),
            block(64, 512),
            block(1024, 512),
            block(9, 256, 512),
            block(9, 128, 512),
            block(9, 256, 512),
            block(9, 256, 512),
            block(9, 256, 512),
            pltpu.VMEM((9, 256, 1), F32),
            block(9, 256, 512),
            block(9, 64, 512),
            pltpu.VMEM((256, 16), F32),
            dma((6, 9)),
            dma((6, 9)),
        ],
        compiler_params=pltpu.CompilerParams(collective_id=0, has_side_effects=True, vmem_limit_bytes=63 << 20),
        name="step",
    )(
        grid_lat, mesh_lat, g2m_send[0], aux, halo_lists.reshape(1, 64), proc_send, proc_recv, cotangent, w_grid_send,
        w_grid_recv, w_feat, w_grid_out, row(gain_grid), w_node_in, w_node_out, row(gain_node), w_proc_send, w_proc_recv,
        w_proc_out, row(gain_proc), w_upd_in, w_upd_out, row(gain_upd),
    )
    outs = pl.pallas_call(
        finish_kernel,
        grid=(8,),
        out_shape=[jax.ShapeDtypeStruct((512, 512), F32)] * 6
        + [jax.ShapeDtypeStruct((1024, 512), F32), jax.ShapeDtypeStruct((64, 512), F32)],
        in_specs=[
            pl.BlockSpec((6, 1, 1, 4, 4, 16, 128), lambda i: (0, i // 4, lax.rem(i, 4), 0, 0, 0, 0)),
            pl.BlockSpec((128, 512), lambda i: (i, 0)),
            pl.BlockSpec((512, 512), lambda i: (0, 0)),
            pl.BlockSpec((8, 512), lambda i: (i, 0)),
        ],
        out_specs=[pl.BlockSpec((64, 512), lambda i: (i, 0))] * 6
        + [pl.BlockSpec((128, 512), lambda i: (i, 0)), pl.BlockSpec((8, 512), lambda i: (i, 0))],
        name="finish",
    )(full, d_terms, w_grid_send, mesh_new)
    grid_send, grid_recv, grid_out, proc_out, proc_recv_g, proc_send_g, grid_grad, mesh_final = outs
    return mesh_final, grid_grad, grid_send, grid_recv, grid_out, proc_send_g, proc_recv_g, proc_out


def solution(mesh):
    placed = (
        P(("lat", "lon"), None),
        P(("lat", "lon"), None),
        P(("lat", "lon"), None, None),
        P(("lat", "lon"), None, None),
        P(("lat", "lon"), None, None),
        P(("lat", "lon"), None, None),
        P(("lat", "lon"), None),
        P(("lat", "lon"), None),
        P(("lat", "lon"), None),
        P(),
        P(),
        P(),
        P(),
        P(),
        P(),
        P(),
        P(),
        P(),
        P(),
        P(),
        P(),
        P(),
        P(),
        P(),
    )
    return jax.shard_map(
        local,
        mesh=mesh,
        in_specs=placed,
        out_specs=(P(("lat", "lon"), None), P(("lat", "lon"), None), P(), P(), P(), P(), P(), P()),
        check_vma=False,
    )
```

```python
import functools

import jax
import jax.numpy as jnp
from jax import lax
from jax.experimental import pallas as pl
from jax.experimental.pallas import tpu as pltpu
from jax.sharding import PartitionSpec as P

EPSILON = 1e-05
MESH = pl.DeviceIdType.MESH
ORDERS = ((0, 1, 2), (1, 2, 0), (2, 0, 1))
BF = jnp.bfloat16
F32 = jnp.float32


def mm(a, b):
    return jnp.dot(a, b, preferred_element_type=F32)


def mm_t(a, b):
    return lax.dot_general(a, b, (((0,), (0,)), ((), ())), preferred_element_type=F32)


def mm_nt(a, b):
    return lax.dot_general(a, b, (((1,), (1,)), ((), ())), preferred_element_type=F32)


def tail_forward(pre, weight):
    sig = jax.nn.sigmoid(pre)
    hid = (pre * sig).astype(BF)
    z = mm(hid, weight)
    centre = z - jnp.mean(z, axis=-1, keepdims=True)
    inv = lax.rsqrt(jnp.mean(centre * centre, axis=-1, keepdims=True) + EPSILON)
    return hid, centre * inv, inv, sig + pre * sig * (1.0 - sig)


def tail_backward(grad, gain, zhat, inv, slope, weight):
    u = grad * gain
    m1 = jnp.mean(u, axis=-1, keepdims=True)
    m2 = jnp.mean(u * zhat, axis=-1, keepdims=True)
    dz = (inv * (u - m1 - zhat * m2)).astype(BF)
    return dz, mm_nt(dz, weight) * slope


def coordinates():
    lon = lax.axis_index("lon")
    return (lax.axis_index("lat"), lon // 8, lax.rem(lon // 2, 4), lax.rem(lon, 2))


def device(z, x, y, c):
    return (z, (x * 4 + y) * 2 + c)


def ring_peer(me, dim, step):
    spot = list(me)
    spot[dim] = lax.rem(me[dim] + step, 4)
    return device(*spot)


def core_peer(me):
    return device(me[0], me[1], me[2], 1 - me[3])


def tile_peer(dlat, dlon):
    return (lax.rem(lax.axis_index("lat") + dlat + 4, 4), lax.rem(lax.axis_index("lon") + dlon + 32, 32))


def offset_peer(k, sign):
    return tile_peer(sign * (k // 3 - 1), sign * (lax.rem(k, 3) - 1))


def greet(peers):
    barrier = pltpu.get_barrier_semaphore()
    for peer in peers:
        pl.semaphore_signal(barrier, inc=1, device_id=peer, device_id_type=MESH)
    return barrier, len(peers)


def push(src, dst, send, recv, peer):
    return pltpu.make_async_remote_copy(
        src_ref=src, dst_ref=dst, send_sem=send, recv_sem=recv, device_id=peer, device_id_type=MESH
    )


class Reduction:
    def __init__(self, order, source, bufs, send, recv):
        self.order, self.source = ORDERS[order], source
        self.s0, self.r0, self.s1, self.r1, self.e2, self.e3, self.full = bufs
        self.send, self.recv = send, recv

    def copy(self, slot):
        me = coordinates()
        a, b, c = [me[d] for d in self.order]
        step = (slot - 1) % 3 + 1
        if slot == 0:
            src, dst, peer = self.s0, self.r0, core_peer(me)
        elif slot < 4:
            src, dst = self.s1.at[lax.rem(a + step, 4)], self.r1.at[step - 1]
            peer = ring_peer(me, self.order[0], step)
        elif slot < 7:
            src = dst = self.e2.at[b]
            peer = ring_peer(me, self.order[1], step)
        elif slot < 10:
            src = dst = self.e3.at[c]
            peer = ring_peer(me, self.order[2], step)
        elif slot < 13:
            src = dst = self.full.at[me[3], a]
            peer = ring_peer(me, self.order[0], step)
        else:
            src = dst = self.full.at[me[3]]
            peer = core_peer(me)
        return push(src, dst, self.send.at[slot], self.recv.at[slot], peer)

    def arrive(self, base):
        for k in range(3):
            self.copy(base + k).wait_recv()

    def depart(self, base):
        for step in (1, 3, 2):
            self.copy(base + step - 1).start()

    def begin(self):
        other = pl.multiple_of((1 - coordinates()[3]) * 128, 128)
        self.s0[...] = self.source[pl.ds(other, 128), :].astype(BF)
        self.copy(0).start()

    def stage(self, level):
        me = coordinates()
        a, b, c = [me[d] for d in self.order]
        if level == 0:
            self.copy(0).wait_recv()
            mine = pl.multiple_of(me[3] * 128, 128)
            total = self.source[pl.ds(mine, 128), :] + self.r0[...].astype(F32)
            self.s1[...] = total.astype(BF).reshape(4, 32, 512)
            self.depart(1)
        elif level == 1:
            self.arrive(1)
            total = self.s1[a].astype(F32)
            for k in range(3):
                total = total + self.r1[k].astype(F32)
            self.e2[b] = total.astype(BF)
            self.depart(4)
        elif level == 2:
            self.arrive(4)
            self.e3[c] = total_of(self.e2).astype(BF)
            self.depart(7)
        elif level == 3:
            self.arrive(7)
            self.full[me[3], a] = total_of(self.e3).astype(BF)
            self.depart(10)
        else:
            self.arrive(10)
            self.copy(13).start()

    def finish(self):
        self.copy(13).wait_recv()
        for slot in range(14):
            self.copy(slot).wait_send()


def total_of(ref):
    return (ref[0].astype(F32) + ref[1].astype(F32)) + (ref[2].astype(F32) + ref[3].astype(F32))


def reduction_scratch(count):
    shapes = ((128, 512), (128, 512), (4, 32, 512), (3, 32, 512), (4, 32, 512), (4, 32, 512))
    return [pltpu.VMEM((count,) + s, BF) for s in shapes]


OWN = 4


REMOTE = (1, 7, 3, 5, 0, 6, 2, 8)


def main_kernel(*refs):
    (mesh_lat, send_rows, recv_rows, feat, halo_rows, from_row, to_row, cot, w_feat, gain_grid, gain_node, gain_proc,
     gain_upd) = refs[:13]
    stored = refs[13:24]
    full, d_terms, mesh_out = refs[24:27]
    red = refs[27:33]
    held = refs[33:44]
    (red_send, red_recv, grads, mesh_in, index_in, feat_in, part_out, part_in, dsum_out, dsum_in, halo_out, table, back_out,
     back_in, x_s, slots, hid_s, zhat_s, slope_s, inv_s, dpre_s, drecv_s, cols, ex_send, ex_recv, load) = refs[44:]
    (grid_lat, w_grid_send, w_grid_recv, w_grid_out, w_node_in, w_node_out, w_proc_send, w_proc_recv, w_proc_out, w_upd_in,
     w_upd_out) = held
    loads = [pltpu.make_async_copy(stored[n], held[n], load.at[n]) for n in range(11)]
    for copy in loads[:2]:
        copy.start()
    me = coordinates()
    barrier, greeted = greet([offset_peer(k, 1) for k in range(9) if k != OWN] + [core_peer(me)] + [ring_peer(me, d, s) for d in range(3) for s in (1, 2, 3)])

    def mesh_copy(k):
        return push(mesh_lat, mesh_in.at[k], ex_send.at[0, k], ex_recv.at[0, k], offset_peer(k, -1))

    def index_copy(k):
        return push(recv_rows.at[k], index_in.at[k], ex_send.at[1, k], ex_recv.at[1, k], offset_peer(k, -1))

    def feat_copy(k):
        return push(feat.at[k], feat_in.at[k], ex_send.at[6, k], ex_recv.at[6, k], offset_peer(k, -1))

    def part_copy(k):
        return push(part_out.at[k], part_in.at[k], ex_send.at[2, k], ex_recv.at[2, k], offset_peer(k, 1))

    def dsum_copy(k):
        return push(dsum_out, dsum_in.at[k], ex_send.at[3, k], ex_recv.at[3, k], offset_peer(k, -1))

    ways = ((1, 0), (-1, 0), (0, 1), (0, -1))

    def halo_copy(j):
        return push(halo_out.at[pl.ds(16 * j, 16)], table.at[pl.ds(64 + 16 * j, 16)], ex_send.at[4, j], ex_recv.at[4, j], tile_peer(*ways[j]))

    def back_copy(j):
        dlat, dlon = ways[j]
        return push(back_out.at[pl.ds(16 * j, 16)], back_in.at[pl.ds(16 * j, 16)], ex_send.at[5, j], ex_recv.at[5, j], tile_peer(-dlat, -dlon))

    def each(copy):
        for k in REMOTE:
            copy(k).start()

    loads[0].wait()
    loads[1].wait()
    padded = jnp.concatenate([send_rows[k] for k in range(9)] + [jnp.zeros((7, 256), jnp.int32)], axis=0).astype(F32)
    cols[...] = jnp.transpose(padded)

    def slots_body(k, carry):
        lane = lax.broadcasted_iota(jnp.int32, (256, 16), 1)
        col = jnp.sum(jnp.where(lane == k, cols[...], 0.0), axis=1, keepdims=True).astype(jnp.int32)
        pick = (col == lax.broadcasted_iota(jnp.int32, (256, 1024), 1)).astype(F32).astype(BF)
        x = mm(pick, grid_lat[...]).astype(BF)
        x_s[k] = x
        slots[k] = mm(x, w_grid_send[...]).astype(BF)
        return carry

    lax.fori_loop(0, 3, slots_body, 0)
    pl.semaphore_wait(barrier, greeted)
    each(index_copy)
    each(feat_copy)
    each(mesh_copy)
    for copy in loads[2:]:
        copy.start()
    mesh_in[OWN] = mesh_lat[...]
    index_in[OWN] = recv_rows[OWN]
    feat_in[OWN] = feat[OWN]
    lax.fori_loop(3, 9, slots_body, 0)
    loads[2].wait()
    loads[3].wait()

    def receivers(k):
        return (index_in[k] == lax.broadcasted_iota(jnp.int32, (64, 256), 0)).astype(F32).astype(BF)

    near, far = 5 - 2 * me[3], 3 + 2 * me[3]
    order = (near, far, 1, 7, 0, 6, 2, 8)

    def forward(k):
        if k is not OWN:
            mesh_copy(k).wait_recv()
            index_copy(k).wait_recv()
            feat_copy(k).wait_recv()
        full_terms = mm(mesh_in[k], w_grid_recv[...])
        high = full_terms.astype(BF)
        low = (full_terms - high.astype(F32)).astype(BF)
        rec = receivers(k)
        left = jnp.concatenate([rec, rec, feat_in[k], jnp.zeros((12, 256), BF)], axis=0)
        right = jnp.concatenate([high, low, w_feat[...], jnp.zeros((12, 512), BF)], axis=0)
        pre = slots[k].astype(F32) + mm_t(left, right)
        hid, zhat, inv, slope = tail_forward(pre, w_grid_out[...])
        hid_s[k], zhat_s[k], slope_s[k] = hid, zhat.astype(BF), slope.astype(BF)
        inv_s[k] = inv
        part_out[k] = (mm(rec, zhat.astype(BF)) * gain_grid[...]).astype(BF)
        if k is not OWN:
            part_copy(k).start()

    for k in order + (OWN,):
        forward(k)

    for copy in loads[4:]:
        copy.wait()
    node_pre = mm(mesh_lat[...], w_node_in[:512, :])
    grid_sum = part_out[OWN].astype(F32)
    for k in (3, 5, 1, 7, 0, 6, 2, 8):
        part_copy(k).wait_recv()
        grid_sum = grid_sum + part_in[k].astype(F32)
    node_pre = node_pre + mm(grid_sum.astype(BF), w_node_in[512:, :])
    node_hid, node_zhat, node_inv, node_slope = tail_forward(node_pre, w_node_out[...])
    state = mesh_lat[...].astype(F32) + node_zhat * gain_node[...]
    state_bf = state.astype(BF)
    own_terms = mm(state_bf, w_proc_send[...]).astype(BF)
    spots = lax.broadcasted_iota(jnp.int32, (64, 16), 0)
    lists = [(halo_rows[j : j + 1, :] == spots).astype(F32).astype(BF) for j in range(4)]
    for j in range(4):
        halo_out[pl.ds(16 * j, 16), :] = mm_t(lists[j], own_terms).astype(BF)
        halo_copy(j).start()
    table[:64, :] = own_terms
    p_recv = mm(state_bf, w_proc_recv[...])
    p_high = p_recv.astype(BF)
    p_low = (p_recv - p_high.astype(F32)).astype(BF)
    pick_from = (from_row[...] == lax.broadcasted_iota(jnp.int32, (128, 512), 0)).astype(F32).astype(BF)
    pick_to = (to_row[...] == lax.broadcasted_iota(jnp.int32, (64, 512), 0)).astype(F32).astype(BF)
    upd_pre = mm(state_bf, w_upd_in[:512, :])
    for j in range(4):
        halo_copy(j).wait_recv()
    left = jnp.concatenate([pick_from, pick_to, pick_to], axis=0)
    right = jnp.concatenate([table[...], p_high, p_low], axis=0)
    proc_pre = mm_t(left, right)
    p_hid, p_zhat, p_inv, p_slope = tail_forward(proc_pre, w_proc_out[...])
    proc_sum = mm(pick_to, p_zhat.astype(BF)) * gain_proc[...]
    upd_pre = upd_pre + mm(proc_sum.astype(BF), w_upd_in[512:, :])
    upd_hid, upd_zhat, upd_inv, upd_slope = tail_forward(upd_pre, w_upd_out[...])
    mesh_out[...] = state + upd_zhat * gain_upd[...]
    top = cot[...].astype(F32)
    d_upd = tail_backward(top, gain_upd[...], upd_zhat, upd_inv, upd_slope, w_upd_out[...])[1].astype(BF)
    d_sum = mm_nt(d_upd, w_upd_in[512:, :])
    d_state = top + mm_nt(d_upd, w_upd_in[:512, :])
    d_msg = mm_t(pick_to, d_sum.astype(BF))
    dz, d_pre = tail_backward(d_msg, gain_proc[...], p_zhat, p_inv, p_slope, w_proc_out[...])
    d_pre = d_pre.astype(BF)
    d_table = mm(pick_from, d_pre)
    back_out[...] = d_table[64:, :].astype(BF)
    for j in range(4):
        back_copy(j).start()
    d_recv2 = mm(pick_to, d_pre).astype(BF)
    d_state = d_state + mm_nt(d_recv2, w_proc_recv[...])
    grads[3] = mm_t(p_hid, dz)
    grads[4] = mm_t(state_bf, d_recv2)
    for j in range(4):
        back_copy(j).wait_recv()
    d_own = d_table[:64, :]
    for j in range(4):
        d_own = d_own + mm(lists[j], back_in[pl.ds(16 * j, 16), :])
    d_own = d_own.astype(BF)
    d_state = d_state + mm_nt(d_own, w_proc_send[...])
    d_node = tail_backward(d_state, gain_node[...], node_zhat, node_inv, node_slope, w_node_out[...])[1].astype(BF)
    dsum_out[...] = mm_nt(d_node, w_node_in[512:, :]).astype(BF)
    each(dsum_copy)
    dsum_in[OWN] = dsum_out[...]
    grads[5] = mm_t(state_bf, d_own)
    parts = []
    for n in range(12):
        g, half = n // 2, n % 2
        bufs = [b.at[n] for b in red] + [full.at[g, half]]
        parts.append(Reduction(g % 3, grads.at[g, pl.ds(256 * half, 256)], bufs, red_send.at[n], red_recv.at[n]))
    early = parts[6:]
    for part in early:
        part.begin()

    grads[0] = jnp.zeros((512, 512), F32)
    grads[2] = jnp.zeros((512, 512), F32)
    def backward(k):
        if k is not OWN:
            dsum_copy(k).wait_recv()
        rec = receivers(k)
        grad = mm_t(rec, dsum_in[k])
        zhat = zhat_s[k].astype(F32)
        dz, dpre = tail_backward(grad, gain_grid[...], zhat, inv_s[k], slope_s[k].astype(F32), w_grid_out[...])
        grads[2] += mm_t(hid_s[k], dz)
        dpre = dpre.astype(BF)
        dpre_s[k] = dpre
        grads[0] += mm_t(x_s[k], dpre)
        drecv_s[k] = mm(rec, dpre).astype(BF)

    for n, k in enumerate((OWN,) + order):
        backward(k)
        if n in (1, 5):
            for part in early:
                part.stage(n // 5)
    late = (parts[4], parts[0], parts[5], parts[1], parts[2], parts[3])
    for part in late[:4]:
        part.begin()
    grads[1] = mm_t(mesh_in[...].reshape(576, 512), drecv_s[...].reshape(576, 512))
    for part in late[4:]:
        part.begin()
    every = jnp.concatenate([send_rows[k] for k in range(9)], axis=1)

    def terms_back(i, carry):
        rows = pl.ds(pl.multiple_of(i * 256, 256), 256)
        ids = lax.broadcasted_iota(jnp.int32, (256, 2304), 0) + i * 256
        put = (every == ids).astype(F32).astype(BF)
        d_terms[rows, :] = mm(put, dpre_s[...].reshape(2304, 512)).astype(BF)
        return carry

    def run(group, level):
        for part in group:
            part.stage(level)

    run(late, 0)
    lax.fori_loop(0, 2, terms_back, 0)
    run(early, 2)
    run(late, 1)
    lax.fori_loop(2, 3, terms_back, 0)
    run(early, 3)
    run(late, 2)
    lax.fori_loop(3, 4, terms_back, 0)
    run(early, 4)
    run(late, 3)
    run(late, 4)
    for part in early:
        part.finish()
    for part in late:
        part.finish()
    for k in range(9):
        if k != OWN:
            for copy in (mesh_copy, index_copy, feat_copy, part_copy, dsum_copy):
                copy(k).wait_send()
    for j in range(4):
        halo_copy(j).wait_send()
        back_copy(j).wait_send()


def finish_kernel(full, d_terms, mesh_in, w_grid_send, *refs):
    outs, (weight_v, out_v, grid_v, in_sem, out_sem) = refs[:8], refs[8:]
    load = pltpu.make_async_copy(w_grid_send, weight_v, in_sem)
    load.start()
    done = [pltpu.make_async_copy(mesh_in, outs[7], out_sem.at[10])]
    done[0].start()
    for g in range(6):

        def spread(i, carry, g=g):
            out_v[g, pl.ds(pl.multiple_of(i * 32, 32), 32), :] = full[g, i // 8, lax.rem(i // 4, 2), lax.rem(i, 4)].astype(F32)
            return carry

        lax.fori_loop(0, 16, spread, 0)
        done.append(pltpu.make_async_copy(out_v.at[g], outs[g], out_sem.at[g]))
        done[-1].start()
        if g == 1:
            load.wait()
        if g >= 1 and g < 5:
            rows = pl.ds(256 * (g - 1), 256)
            grid_v[rows, :] = mm_nt(d_terms[rows, :], weight_v[...])
            done.append(pltpu.make_async_copy(grid_v.at[rows], outs[6].at[rows], out_sem.at[5 + g]))
            done[-1].start()
    for copy in done:
        copy.wait()


def local(
    grid_lat,
    mesh_lat,
    g2m_send,
    g2m_recv,
    g2m_feat,
    halo_lists,
    proc_send,
    proc_recv,
    cotangent,
    w_grid_send,
    w_grid_recv,
    w_grid_feat,
    w_grid_out,
    gain_grid,
    w_node_in,
    w_node_out,
    gain_node,
    w_proc_send,
    w_proc_recv,
    w_proc_out,
    gain_proc,
    w_upd_in,
    w_upd_out,
    gain_upd,
):
    feat = g2m_feat[0].reshape(4, 9, 256).transpose(1, 0, 2)
    send_rows = g2m_send.transpose(1, 0, 2)
    recv_rows = g2m_recv.transpose(1, 0, 2)
    row = lambda gain: gain.reshape(1, 512)
    vmem = pl.BlockSpec(memory_space=pltpu.VMEM)
    dma = pltpu.SemaphoreType.DMA
    block = lambda *shape: pltpu.VMEM(shape, BF)
    full, d_terms, mesh_new = pl.pallas_call(
        main_kernel,
        out_shape=[
            pltpu.VMEM((6, 2, 2, 4, 32, 512), BF),
            pltpu.VMEM((1024, 512), BF),
            pltpu.VMEM((64, 512), F32),
        ],
        in_specs=[vmem] * 13 + [pl.BlockSpec(memory_space=pl.ANY)] * 11,
        out_specs=[vmem] * 3,
        scratch_shapes=reduction_scratch(12)
        + [block(1024, 512), block(512, 512), block(512, 512), block(512, 512), block(1024, 512)]
        + [block(512, 512)] * 4
        + [block(1024, 512), block(512, 512)]
        + [
            dma((12, 14)),
            dma((12, 14)),
            pltpu.VMEM((6, 512, 512), F32),
            block(9, 64, 512),
            pltpu.VMEM((9, 1, 256), jnp.int32),
            block(9, 4, 256),
            block(9, 64, 512),
            block(9, 64, 512),
            block(64, 512),
            block(9, 64, 512),
            block(64, 512),
            block(128, 512),
            block(64, 512),
            block(64, 512),
            block(9, 256, 512),
            block(9, 256, 512),
            block(9, 256, 512),
            block(9, 256, 512),
            block(9, 256, 512),
            pltpu.VMEM((9, 256, 1), F32),
            block(9, 256, 512),
            block(9, 64, 512),
            pltpu.VMEM((256, 16), F32),
            dma((7, 9)),
            dma((7, 9)),
            dma((11,)),
        ],
        compiler_params=pltpu.CompilerParams(collective_id=0, has_side_effects=True, vmem_limit_bytes=59 << 20),
        name="step",
    )(
        mesh_lat, send_rows, recv_rows, feat, halo_lists[0], proc_send, proc_recv, cotangent, w_grid_feat, row(gain_grid),
        row(gain_node), row(gain_proc), row(gain_upd), grid_lat, w_grid_send, w_grid_recv, w_grid_out, w_node_in, w_node_out,
        w_proc_send, w_proc_recv, w_proc_out, w_upd_in, w_upd_out,
    )
    outs = pl.pallas_call(
        finish_kernel,
        out_shape=[jax.ShapeDtypeStruct((512, 512), F32)] * 6
        + [jax.ShapeDtypeStruct((1024, 512), F32), jax.ShapeDtypeStruct((64, 512), F32)],
        in_specs=[vmem] * 3 + [pl.BlockSpec(memory_space=pl.ANY)],
        out_specs=[pl.BlockSpec(memory_space=pl.ANY)] * 8,
        scratch_shapes=[
            block(512, 512),
            pltpu.VMEM((6, 512, 512), F32),
            pltpu.VMEM((1024, 512), F32),
            dma,
            dma((11,)),
        ],
        compiler_params=pltpu.CompilerParams(vmem_limit_bytes=40 << 20),
        name="finish",
    )(full, d_terms, mesh_new, w_grid_send)
    grid_send, grid_recv, grid_out, proc_out, proc_recv_g, proc_send_g, grid_grad, mesh_final = outs
    return mesh_final, grid_grad, grid_send, grid_recv, grid_out, proc_send_g, proc_recv_g, proc_out


def solution(mesh):
    placed = (
        P(("lat", "lon"), None),
        P(("lat", "lon"), None),
        P(("lat", "lon"), None, None),
        P(("lat", "lon"), None, None),
        P(("lat", "lon"), None, None),
        P(("lat", "lon"), None, None),
        P(("lat", "lon"), None),
        P(("lat", "lon"), None),
        P(("lat", "lon"), None),
        P(),
        P(),
        P(),
        P(),
        P(),
        P(),
        P(),
        P(),
        P(),
        P(),
        P(),
        P(),
        P(),
        P(),
        P(),
    )
    return jax.shard_map(
        local,
        mesh=mesh,
        in_specs=placed,
        out_specs=(P(("lat", "lon"), None), P(("lat", "lon"), None), P(), P(), P(), P(), P(), P()),
        check_vma=False,
    )
```

```python
import functools

import jax
import jax.numpy as jnp
from jax import lax
from jax.experimental import pallas as pl
from jax.experimental.pallas import tpu as pltpu
from jax.sharding import PartitionSpec as P

EPSILON = 1e-05
MESH = pl.DeviceIdType.MESH
ORDERS = ((0, 1, 2), (1, 2, 0), (2, 0, 1))
BF = jnp.bfloat16
F32 = jnp.float32


def mm(a, b):
    return jnp.dot(a, b, preferred_element_type=F32)


def mm_t(a, b):
    return lax.dot_general(a, b, (((0,), (0,)), ((), ())), preferred_element_type=F32)


def mm_nt(a, b):
    return lax.dot_general(a, b, (((1,), (1,)), ((), ())), preferred_element_type=F32)


def tail_forward(pre, weight):
    sig = jax.nn.sigmoid(pre)
    hid = (pre * sig).astype(BF)
    z = mm(hid, weight)
    centre = z - jnp.mean(z, axis=-1, keepdims=True)
    inv = lax.rsqrt(jnp.mean(centre * centre, axis=-1, keepdims=True) + EPSILON)
    return hid, centre * inv, inv, sig + pre * sig * (1.0 - sig)


def tail_backward(grad, gain, zhat, inv, slope, weight):
    u = grad * gain
    m1 = jnp.mean(u, axis=-1, keepdims=True)
    m2 = jnp.mean(u * zhat, axis=-1, keepdims=True)
    dz = (inv * (u - m1 - zhat * m2)).astype(BF)
    return dz, mm_nt(dz, weight) * slope


def coordinates():
    lon = lax.axis_index("lon")
    return (lax.axis_index("lat"), lon // 8, lax.rem(lon // 2, 4), lax.rem(lon, 2))


def device(z, x, y, c):
    return (z, (x * 4 + y) * 2 + c)


def ring_peer(me, dim, step):
    spot = list(me)
    spot[dim] = lax.rem(me[dim] + step, 4)
    return device(*spot)


def core_peer(me):
    return device(me[0], me[1], me[2], 1 - me[3])


def tile_peer(dlat, dlon):
    return (lax.rem(lax.axis_index("lat") + dlat + 4, 4), lax.rem(lax.axis_index("lon") + dlon + 32, 32))


def offset_peer(k, sign):
    return tile_peer(sign * (k // 3 - 1), sign * (lax.rem(k, 3) - 1))


def greet(peers):
    barrier = pltpu.get_barrier_semaphore()
    for peer in peers:
        pl.semaphore_signal(barrier, inc=1, device_id=peer, device_id_type=MESH)
    return barrier, len(peers)


def push(src, dst, send, recv, peer):
    return pltpu.make_async_remote_copy(
        src_ref=src, dst_ref=dst, send_sem=send, recv_sem=recv, device_id=peer, device_id_type=MESH
    )


class Reduction:
    def __init__(self, order, source, bufs, send, recv, sized):
        self.sized = sized
        self.order, self.source = ORDERS[order], source
        self.s0, self.r0, self.s1, self.r1, self.e2, self.e3, self.full = bufs
        self.send, self.recv = send, recv

    def copy(self, slot):
        me = coordinates()
        a, b, c = [me[d] for d in self.order]
        step = (slot - 1) % 3 + 1
        if slot == 0:
            src, dst, peer = self.s0, self.r0, core_peer(me)
        elif slot < 4:
            src, dst = self.s1.at[lax.rem(a + step, 4)], self.r1.at[step - 1]
            peer = ring_peer(me, self.order[0], step)
        elif slot < 7:
            src = dst = self.e2.at[b]
            peer = ring_peer(me, self.order[1], step)
        elif slot < 10:
            src = dst = self.e3.at[c]
            peer = ring_peer(me, self.order[2], step)
        elif slot < 13:
            src = dst = self.full.at[me[3], a]
            peer = ring_peer(me, self.order[0], step)
        else:
            src = dst = self.full.at[me[3]]
            peer = core_peer(me)
        return push(src, dst, self.send, self.recv.at[(slot + 2) // 3], peer)

    def wait_for(self, group, ref):
        push(ref, ref, self.send, self.recv.at[group], core_peer(coordinates())).wait_recv()

    def depart(self, base):
        for step in (1, 3, 2):
            self.copy(base + step - 1).start()

    def begin(self):
        other = pl.multiple_of((1 - coordinates()[3]) * 128, 128)
        self.s0[...] = self.source[pl.ds(other, 128), :].astype(BF)
        self.copy(0).start()

    def stage(self, level):
        me = coordinates()
        a, b, c = [me[d] for d in self.order]
        if level == 0:
            self.wait_for(0, self.r0)
            mine = pl.multiple_of(me[3] * 128, 128)
            total = self.source[pl.ds(mine, 128), :] + self.r0[...].astype(F32)
            self.s1[...] = total.astype(BF).reshape(4, 32, 512)
            self.depart(1)
        elif level == 1:
            self.wait_for(1, self.r1)
            total = self.s1[a].astype(F32)
            for k in range(3):
                total = total + self.r1[k].astype(F32)
            self.e2[b] = total.astype(BF)
            self.depart(4)
        elif level == 2:
            self.wait_for(2, self.e2.at[pl.ds(0, 3)])
            self.e3[c] = total_of(self.e2).astype(BF)
            self.depart(7)
        elif level == 3:
            self.wait_for(3, self.e3.at[pl.ds(0, 3)])
            self.full[me[3], a] = total_of(self.e3).astype(BF)
            self.depart(10)
        else:
            self.wait_for(4, self.full.at[0, pl.ds(0, 3)])
            self.copy(13).start()

    def finish(self):
        self.wait_for(5, self.full.at[0])
        push(self.sized, self.sized, self.send, self.recv.at[0], core_peer(coordinates())).wait_send()


def total_of(ref):
    return (ref[0].astype(F32) + ref[1].astype(F32)) + (ref[2].astype(F32) + ref[3].astype(F32))


def reduction_scratch(count):
    shapes = ((128, 512), (128, 512), (4, 32, 512), (3, 32, 512), (4, 32, 512), (4, 32, 512))
    return [pltpu.VMEM((count,) + s, BF) for s in shapes]


OWN = 4


REMOTE = (1, 7, 3, 5, 0, 6, 2, 8)


def main_kernel(*refs):
    stored, (full, d_terms, mesh_out), red, held = refs[:24], refs[24:27], refs[27:33], refs[33:57]
    (red_send, red_recv, grads, mesh_in, index_in, feat_in, part_out, part_in, dsum_out, dsum_in, halo_out, table, back_out,
     back_in, x_s, slots, hid_s, zhat_s, slope_s, inv_s, dpre_s, drecv_s, cols, ex_send, ex_recv, ex_all, load) = refs[57:]
    (send_rows, grid_lat, w_grid_send, mesh_lat, recv_rows, feat, w_grid_recv, w_grid_out, w_feat, gain_grid, w_node_in,
     w_node_out, gain_node, w_proc_send, w_proc_recv, halo_rows, from_row, to_row, w_proc_out, gain_proc, w_upd_in, w_upd_out,
     gain_upd, cot) = held
    loads = [pltpu.make_async_copy(stored[n], held[n], load.at[n]) for n in range(24)]
    for copy in loads[:6]:
        copy.start()
    me = coordinates()
    barrier, greeted = greet([offset_peer(k, 1) for k in range(9) if k != OWN] + [core_peer(me)] + [ring_peer(me, d, s) for d in range(3) for s in (1, 2, 3)])

    def mesh_copy(k):
        return push(mesh_lat, mesh_in.at[k], ex_send.at[0], ex_recv.at[0, k], offset_peer(k, -1))

    def index_copy(k):
        return push(recv_rows.at[k], index_in.at[k], ex_send.at[1], ex_recv.at[1, k], offset_peer(k, -1))

    def feat_copy(k):
        return push(feat.at[k], feat_in.at[k], ex_send.at[2], ex_recv.at[2, k], offset_peer(k, -1))

    def part_copy(k):
        return push(part_out.at[k], part_in.at[k], ex_send.at[4], ex_all.at[0], offset_peer(k, 1))

    def dsum_copy(k):
        return push(dsum_out, dsum_in.at[k], ex_send.at[3], ex_recv.at[3, k], offset_peer(k, -1))

    ways = ((1, 0), (-1, 0), (0, 1), (0, -1))

    def halo_copy(j):
        return push(halo_out.at[pl.ds(16 * j, 16)], table.at[pl.ds(64 + 16 * j, 16)], ex_send.at[5], ex_all.at[1], tile_peer(*ways[j]))

    def back_copy(j):
        dlat, dlon = ways[j]
        return push(back_out.at[pl.ds(16 * j, 16)], back_in.at[pl.ds(16 * j, 16)], ex_send.at[6], ex_all.at[2], tile_peer(-dlat, -dlon))

    def landed(ref, n):
        push(ref, ref, ex_send.at[0], ex_all.at[n], core_peer(me)).wait_recv()

    def each(copy):
        for k in REMOTE:
            copy(k).start()

    for copy in loads[:3]:
        copy.wait()
    padded = jnp.concatenate([send_rows[k] for k in range(9)] + [jnp.zeros((7, 256), jnp.int32)], axis=0).astype(F32)
    cols[...] = jnp.transpose(padded)

    def slots_body(k, carry):
        lane = lax.broadcasted_iota(jnp.int32, (256, 16), 1)
        col = jnp.sum(jnp.where(lane == k, cols[...], 0.0), axis=1, keepdims=True).astype(jnp.int32)
        pick = (col == lax.broadcasted_iota(jnp.int32, (256, 1024), 1)).astype(F32).astype(BF)
        x = mm(pick, grid_lat[...]).astype(BF)
        x_s[k] = x
        slots[k] = mm(x, w_grid_send[...]).astype(BF)
        return carry

    lax.fori_loop(0, 3, slots_body, 0)
    for copy in loads[3:6]:
        copy.wait()
    pl.semaphore_wait(barrier, greeted)
    each(index_copy)
    each(feat_copy)
    each(mesh_copy)
    for copy in loads[6:]:
        copy.start()
    mesh_in[OWN] = mesh_lat[...]
    index_in[OWN] = recv_rows[OWN]
    feat_in[OWN] = feat[OWN]
    lax.fori_loop(3, 9, slots_body, 0)
    for copy in loads[6:10]:
        copy.wait()

    def receivers(k):
        return (index_in[k] == lax.broadcasted_iota(jnp.int32, (64, 256), 0)).astype(F32).astype(BF)

    near, far = 5 - 2 * me[3], 3 + 2 * me[3]
    order = (near, far, 1, 7, 0, 6, 2, 8)

    def forward(k):
        if k is not OWN:
            mesh_copy(k).wait_recv()
            index_copy(k).wait_recv()
            feat_copy(k).wait_recv()
        full_terms = mm(mesh_in[k], w_grid_recv[...])
        high = full_terms.astype(BF)
        low = (full_terms - high.astype(F32)).astype(BF)
        rec = receivers(k)
        left = jnp.concatenate([rec, rec, feat_in[k], jnp.zeros((12, 256), BF)], axis=0)
        right = jnp.concatenate([high, low, w_feat[...], jnp.zeros((12, 512), BF)], axis=0)
        pre = slots[k].astype(F32) + mm_t(left, right)
        hid, zhat, inv, slope = tail_forward(pre, w_grid_out[...])
        hid_s[k], zhat_s[k], slope_s[k] = hid, zhat.astype(BF), slope.astype(BF)
        inv_s[k] = inv
        part_out[k] = (mm(rec, zhat.astype(BF)) * gain_grid[...]).astype(BF)
        if k is not OWN:
            part_copy(k).start()

    for k in order + (OWN,):
        forward(k)

    for copy in loads[10:]:
        copy.wait()
    node_pre = mm(mesh_lat[...], w_node_in[:512, :])
    grid_sum = part_out[OWN].astype(F32)
    landed(part_in.at[pl.ds(0, 8)], 0)
    for k in REMOTE:
        grid_sum = grid_sum + part_in[k].astype(F32)
    node_pre = node_pre + mm(grid_sum.astype(BF), w_node_in[512:, :])
    node_hid, node_zhat, node_inv, node_slope = tail_forward(node_pre, w_node_out[...])
    state = mesh_lat[...].astype(F32) + node_zhat * gain_node[...]
    state_bf = state.astype(BF)
    own_terms = mm(state_bf, w_proc_send[...]).astype(BF)
    spots = lax.broadcasted_iota(jnp.int32, (64, 16), 0)
    lists = [(halo_rows[j : j + 1, :] == spots).astype(F32).astype(BF) for j in range(4)]
    for j in range(4):
        halo_out[pl.ds(16 * j, 16), :] = mm_t(lists[j], own_terms).astype(BF)
        halo_copy(j).start()
    table[:64, :] = own_terms
    p_recv = mm(state_bf, w_proc_recv[...])
    p_high = p_recv.astype(BF)
    p_low = (p_recv - p_high.astype(F32)).astype(BF)
    pick_from = (from_row[...] == lax.broadcasted_iota(jnp.int32, (128, 512), 0)).astype(F32).astype(BF)
    pick_to = (to_row[...] == lax.broadcasted_iota(jnp.int32, (64, 512), 0)).astype(F32).astype(BF)
    upd_pre = mm(state_bf, w_upd_in[:512, :])
    landed(table.at[pl.ds(64, 64)], 1)
    left = jnp.concatenate([pick_from, pick_to, pick_to], axis=0)
    right = jnp.concatenate([table[...], p_high, p_low], axis=0)
    proc_pre = mm_t(left, right)
    p_hid, p_zhat, p_inv, p_slope = tail_forward(proc_pre, w_proc_out[...])
    proc_sum = mm(pick_to, p_zhat.astype(BF)) * gain_proc[...]
    upd_pre = upd_pre + mm(proc_sum.astype(BF), w_upd_in[512:, :])
    upd_hid, upd_zhat, upd_inv, upd_slope = tail_forward(upd_pre, w_upd_out[...])
    mesh_out[...] = state + upd_zhat * gain_upd[...]
    top = cot[...].astype(F32)
    d_upd = tail_backward(top, gain_upd[...], upd_zhat, upd_inv, upd_slope, w_upd_out[...])[1].astype(BF)
    d_sum = mm_nt(d_upd, w_upd_in[512:, :])
    d_state = top + mm_nt(d_upd, w_upd_in[:512, :])
    d_msg = mm_t(pick_to, d_sum.astype(BF))
    dz, d_pre = tail_backward(d_msg, gain_proc[...], p_zhat, p_inv, p_slope, w_proc_out[...])
    d_pre = d_pre.astype(BF)
    d_table = mm(pick_from, d_pre)
    back_out[...] = d_table[64:, :].astype(BF)
    for j in range(4):
        back_copy(j).start()
    d_recv2 = mm(pick_to, d_pre).astype(BF)
    d_state = d_state + mm_nt(d_recv2, w_proc_recv[...])
    grads[3] = mm_t(p_hid, dz)
    grads[4] = mm_t(state_bf, d_recv2)
    landed(back_in, 2)
    d_own = d_table[:64, :]
    for j in range(4):
        d_own = d_own + mm(lists[j], back_in[pl.ds(16 * j, 16), :])
    d_own = d_own.astype(BF)
    d_state = d_state + mm_nt(d_own, w_proc_send[...])
    d_node = tail_backward(d_state, gain_node[...], node_zhat, node_inv, node_slope, w_node_out[...])[1].astype(BF)
    dsum_out[...] = mm_nt(d_node, w_node_in[512:, :]).astype(BF)
    each(dsum_copy)
    dsum_in[OWN] = dsum_out[...]
    grads[5] = mm_t(state_bf, d_own)
    parts = []
    for n in range(12):
        g, half = n // 2, n % 2
        bufs = [b.at[n] for b in red] + [full.at[g, half]]
        parts.append(Reduction(g % 3, grads.at[g, pl.ds(256 * half, 256)], bufs, red_send.at[n], red_recv.at[n], red[2].at[pl.ds(0, 5)]))
    early = parts[6:]
    for part in early:
        part.begin()

    grads[0] = jnp.zeros((512, 512), F32)
    grads[2] = jnp.zeros((512, 512), F32)
    def backward(k):
        if k is not OWN:
            dsum_copy(k).wait_recv()
        rec = receivers(k)
        grad = mm_t(rec, dsum_in[k])
        zhat = zhat_s[k].astype(F32)
        dz, dpre = tail_backward(grad, gain_grid[...], zhat, inv_s[k], slope_s[k].astype(F32), w_grid_out[...])
        grads[2] += mm_t(hid_s[k], dz)
        dpre = dpre.astype(BF)
        dpre_s[k] = dpre
        grads[0] += mm_t(x_s[k], dpre)
        drecv_s[k] = mm(rec, dpre).astype(BF)

    for n, k in enumerate((OWN,) + order):
        backward(k)
        if n in (1, 5):
            for part in early:
                part.stage(n // 5)
    late = (parts[4], parts[0], parts[5], parts[1], parts[2], parts[3])
    for part in late[:4]:
        part.begin()
    grads[1] = mm_t(mesh_in[...].reshape(576, 512), drecv_s[...].reshape(576, 512))
    for part in late[4:]:
        part.begin()
    every = jnp.concatenate([send_rows[k] for k in range(9)], axis=1)

    def terms_back(i, carry):
        rows = pl.ds(pl.multiple_of(i * 256, 256), 256)
        ids = lax.broadcasted_iota(jnp.int32, (256, 2304), 0) + i * 256
        put = (every == ids).astype(F32).astype(BF)
        d_terms[rows, :] = mm(put, dpre_s[...].reshape(2304, 512)).astype(BF)
        return carry

    def run(group, level):
        for part in group:
            part.stage(level)

    run(late, 0)
    lax.fori_loop(0, 2, terms_back, 0)
    run(early, 2)
    run(late, 1)
    lax.fori_loop(2, 3, terms_back, 0)
    run(early, 3)
    run(late, 2)
    lax.fori_loop(3, 4, terms_back, 0)
    run(early, 4)
    run(late, 3)
    run(late, 4)
    for part in early:
        part.finish()
    for part in late:
        part.finish()
    sent = (mesh_in, index_in, feat_in, dsum_in, part_in)
    for n, ref in enumerate([r.at[pl.ds(0, 8)] for r in sent] + [table.at[pl.ds(0, 64)], back_in]):
        push(ref, ref, ex_send.at[n], ex_all.at[0], core_peer(me)).wait_send()


def finish_kernel(full, d_terms, mesh_in, w_grid_send, *refs):
    outs, (weight_v, out_v, grid_v, in_sem, out_sem) = refs[:8], refs[8:]
    load = pltpu.make_async_copy(w_grid_send, weight_v, in_sem)
    load.start()
    done = [pltpu.make_async_copy(mesh_in, outs[7], out_sem.at[10])]
    done[0].start()
    for g in range(6):

        def spread(i, carry, g=g):
            out_v[g, pl.ds(pl.multiple_of(i * 32, 32), 32), :] = full[g, i // 8, lax.rem(i // 4, 2), lax.rem(i, 4)].astype(F32)
            return carry

        lax.fori_loop(0, 16, spread, 0)
        done.append(pltpu.make_async_copy(out_v.at[g], outs[g], out_sem.at[g]))
        done[-1].start()
        if g == 1:
            load.wait()
        if g >= 1 and g < 5:
            rows = pl.ds(256 * (g - 1), 256)
            grid_v[rows, :] = mm_nt(d_terms[rows, :], weight_v[...])
            done.append(pltpu.make_async_copy(grid_v.at[rows], outs[6].at[rows], out_sem.at[5 + g]))
            done[-1].start()
    for copy in done:
        copy.wait()


def local(
    grid_lat,
    mesh_lat,
    g2m_send,
    g2m_recv,
    g2m_feat,
    halo_lists,
    proc_send,
    proc_recv,
    cotangent,
    w_grid_send,
    w_grid_recv,
    w_grid_feat,
    w_grid_out,
    gain_grid,
    w_node_in,
    w_node_out,
    gain_node,
    w_proc_send,
    w_proc_recv,
    w_proc_out,
    gain_proc,
    w_upd_in,
    w_upd_out,
    gain_upd,
):
    feat = g2m_feat[0].reshape(4, 9, 256).transpose(1, 0, 2)
    send_rows = g2m_send.transpose(1, 0, 2)
    recv_rows = g2m_recv.transpose(1, 0, 2)
    row = lambda gain: gain.reshape(1, 512)
    vmem = pl.BlockSpec(memory_space=pltpu.VMEM)
    dma = pltpu.SemaphoreType.DMA
    block = lambda *shape: pltpu.VMEM(shape, BF)
    given = (
        send_rows, grid_lat, w_grid_send, mesh_lat, recv_rows, feat, w_grid_recv, w_grid_out, w_grid_feat, row(gain_grid),
        w_node_in, w_node_out, row(gain_node), w_proc_send, w_proc_recv, halo_lists[0], proc_send, proc_recv, w_proc_out,
        row(gain_proc), w_upd_in, w_upd_out, row(gain_upd), cotangent,
    )
    full, d_terms, mesh_new = pl.pallas_call(
        main_kernel,
        out_shape=[
            pltpu.VMEM((6, 2, 2, 4, 32, 512), BF),
            pltpu.VMEM((1024, 512), BF),
            pltpu.VMEM((64, 512), F32),
        ],
        in_specs=[pl.BlockSpec(memory_space=pl.ANY)] * 24,
        out_specs=[vmem] * 3,
        scratch_shapes=reduction_scratch(12)
        + [pltpu.VMEM(value.shape, value.dtype) for value in given]
        + [
            dma((12,)),
            dma((12, 6)),
            pltpu.VMEM((6, 512, 512), F32),
            block(9, 64, 512),
            pltpu.VMEM((9, 1, 256), jnp.int32),
            block(9, 4, 256),
            block(9, 64, 512),
            block(9, 64, 512),
            block(64, 512),
            block(9, 64, 512),
            block(64, 512),
            block(128, 512),
            block(64, 512),
            block(64, 512),
            block(9, 256, 512),
            block(9, 256, 512),
            block(9, 256, 512),
            block(9, 256, 512),
            block(9, 256, 512),
            pltpu.VMEM((9, 256, 1), F32),
            block(9, 256, 512),
            block(9, 64, 512),
            pltpu.VMEM((256, 16), F32),
            dma((7,)),
            dma((4, 9)),
            dma((3,)),
            dma((24,)),
        ],
        compiler_params=pltpu.CompilerParams(collective_id=0, has_side_effects=True, vmem_limit_bytes=59 << 20),
        name="step",
    )(*given)
    outs = pl.pallas_call(
        finish_kernel,
        out_shape=[jax.ShapeDtypeStruct((512, 512), F32)] * 6
        + [jax.ShapeDtypeStruct((1024, 512), F32), jax.ShapeDtypeStruct((64, 512), F32)],
        in_specs=[vmem] * 3 + [pl.BlockSpec(memory_space=pl.ANY)],
        out_specs=[pl.BlockSpec(memory_space=pl.ANY)] * 8,
        scratch_shapes=[
            block(512, 512),
            pltpu.VMEM((6, 512, 512), F32),
            pltpu.VMEM((1024, 512), F32),
            dma,
            dma((11,)),
        ],
        compiler_params=pltpu.CompilerParams(vmem_limit_bytes=40 << 20),
        name="finish",
    )(full, d_terms, mesh_new, w_grid_send)
    grid_send, grid_recv, grid_out, proc_out, proc_recv_g, proc_send_g, grid_grad, mesh_final = outs
    return mesh_final, grid_grad, grid_send, grid_recv, grid_out, proc_send_g, proc_recv_g, proc_out


def solution(mesh):
    placed = (
        P(("lat", "lon"), None),
        P(("lat", "lon"), None),
        P(("lat", "lon"), None, None),
        P(("lat", "lon"), None, None),
        P(("lat", "lon"), None, None),
        P(("lat", "lon"), None, None),
        P(("lat", "lon"), None),
        P(("lat", "lon"), None),
        P(("lat", "lon"), None),
        P(),
        P(),
        P(),
        P(),
        P(),
        P(),
        P(),
        P(),
        P(),
        P(),
        P(),
        P(),
        P(),
        P(),
        P(),
    )
    return jax.shard_map(
        local,
        mesh=mesh,
        in_specs=placed,
        out_specs=(P(("lat", "lon"), None), P(("lat", "lon"), None), P(), P(), P(), P(), P(), P()),
        check_vma=False,
    )
```

```python
import functools

import jax
import jax.numpy as jnp
from jax import lax
from jax.experimental import pallas as pl
from jax.experimental.pallas import tpu as pltpu
from jax.sharding import PartitionSpec as P

EPSILON = 1e-05
MESH = pl.DeviceIdType.MESH
ORDERS = ((0, 1, 2), (1, 2, 0), (2, 0, 1))
BF = jnp.bfloat16
F32 = jnp.float32


def mm(a, b):
    return jnp.dot(a, b, preferred_element_type=F32)


def mm_t(a, b):
    return lax.dot_general(a, b, (((0,), (0,)), ((), ())), preferred_element_type=F32)


def mm_nt(a, b):
    return lax.dot_general(a, b, (((1,), (1,)), ((), ())), preferred_element_type=F32)


def tail_forward(pre, weight):
    sig = jax.nn.sigmoid(pre)
    hid = (pre * sig).astype(BF)
    z = mm(hid, weight)
    centre = z - jnp.mean(z, axis=-1, keepdims=True)
    inv = lax.rsqrt(jnp.mean(centre * centre, axis=-1, keepdims=True) + EPSILON)
    return hid, centre * inv, inv, sig + pre * sig * (1.0 - sig)


def tail_backward(grad, gain, zhat, inv, slope, weight):
    u = grad * gain
    m1 = jnp.mean(u, axis=-1, keepdims=True)
    m2 = jnp.mean(u * zhat, axis=-1, keepdims=True)
    dz = (inv * (u - m1 - zhat * m2)).astype(BF)
    return dz, mm_nt(dz, weight) * slope


def coordinates():
    lon = lax.axis_index("lon")
    return (lax.axis_index("lat"), lon // 8, lax.rem(lon // 2, 4), lax.rem(lon, 2))


def device(z, x, y, c):
    return (z, (x * 4 + y) * 2 + c)


def ring_peer(me, dim, step):
    spot = list(me)
    spot[dim] = lax.rem(me[dim] + step, 4)
    return device(*spot)


def core_peer(me):
    return device(me[0], me[1], me[2], 1 - me[3])


def tile_peer(dlat, dlon):
    return (lax.rem(lax.axis_index("lat") + dlat + 4, 4), lax.rem(lax.axis_index("lon") + dlon + 32, 32))


def offset_peer(k, sign):
    return tile_peer(sign * (k // 3 - 1), sign * (lax.rem(k, 3) - 1))


def greet(peers):
    barrier = pltpu.get_barrier_semaphore()
    for peer in peers:
        pl.semaphore_signal(barrier, inc=1, device_id=peer, device_id_type=MESH)
    return barrier, len(peers)


def push(src, dst, send, recv, peer):
    return pltpu.make_async_remote_copy(
        src_ref=src, dst_ref=dst, send_sem=send, recv_sem=recv, device_id=peer, device_id_type=MESH
    )


class Reduction:
    def __init__(self, order, source, bufs, send, recv, sized):
        self.sized = sized
        self.order, self.source = ORDERS[order], source
        self.s0, self.r0, self.s1, self.r1, self.e2, self.e3, self.full = bufs
        self.send, self.recv = send, recv

    def copy(self, slot):
        me = coordinates()
        a, b, c = [me[d] for d in self.order]
        step = (slot - 1) % 3 + 1
        if slot == 0:
            src, dst, peer = self.s0, self.r0, core_peer(me)
        elif slot < 4:
            src, dst = self.s1.at[lax.rem(a + step, 4)], self.r1.at[step - 1]
            peer = ring_peer(me, self.order[0], step)
        elif slot < 7:
            src = dst = self.e2.at[b]
            peer = ring_peer(me, self.order[1], step)
        elif slot < 10:
            src = dst = self.e3.at[c]
            peer = ring_peer(me, self.order[2], step)
        elif slot < 13:
            src = dst = self.full.at[me[3], a]
            peer = ring_peer(me, self.order[0], step)
        else:
            src = dst = self.full.at[me[3]]
            peer = core_peer(me)
        return push(src, dst, self.send, self.recv.at[(slot + 2) // 3], peer)

    def wait_for(self, group, ref):
        push(ref, ref, self.send, self.recv.at[group], core_peer(coordinates())).wait_recv()

    def depart(self, base):
        for step in (1, 3, 2):
            self.copy(base + step - 1).start()

    def begin(self):
        other = pl.multiple_of((1 - coordinates()[3]) * 128, 128)
        self.s0[...] = self.source[pl.ds(other, 128), :].astype(BF)
        self.copy(0).start()

    def stage(self, level):
        me = coordinates()
        a, b, c = [me[d] for d in self.order]
        if level == 0:
            self.wait_for(0, self.r0)
            mine = pl.multiple_of(me[3] * 128, 128)
            total = self.source[pl.ds(mine, 128), :] + self.r0[...].astype(F32)
            self.s1[...] = total.astype(BF).reshape(4, 32, 512)
            self.depart(1)
        elif level == 1:
            self.wait_for(1, self.r1)
            total = self.s1[a].astype(F32)
            for k in range(3):
                total = total + self.r1[k].astype(F32)
            self.e2[b] = total.astype(BF)
            self.depart(4)
        elif level == 2:
            self.wait_for(2, self.e2.at[pl.ds(0, 3)])
            self.e3[c] = total_of(self.e2).astype(BF)
            self.depart(7)
        elif level == 3:
            self.wait_for(3, self.e3.at[pl.ds(0, 3)])
            self.full[me[3], a] = total_of(self.e3).astype(BF)
            self.depart(10)
        else:
            self.wait_for(4, self.full.at[0, pl.ds(0, 3)])
            self.copy(13).start()

    def finish(self):
        self.wait_for(5, self.full.at[0])
        push(self.sized, self.sized, self.send, self.recv.at[0], core_peer(coordinates())).wait_send()


def total_of(ref):
    return (ref[0].astype(F32) + ref[1].astype(F32)) + (ref[2].astype(F32) + ref[3].astype(F32))


def reduction_scratch(count):
    shapes = ((128, 512), (128, 512), (4, 32, 512), (3, 32, 512), (4, 32, 512), (4, 32, 512))
    return [pltpu.VMEM((count,) + s, BF) for s in shapes]


OWN = 4


REMOTE = (1, 7, 3, 5, 0, 6, 2, 8)


def main_kernel(*refs):
    stored, (full, d_terms, mesh_out), red, held = refs[:24], refs[24:27], refs[27:33], refs[33:57]
    (red_send, red_recv, grads, mesh_in, index_in, feat_in, part_out, part_in, dsum_out, dsum_in, halo_out, table, back_out,
     back_in, x_s, slots, hid_s, zhat_s, slope_s, inv_s, dpre_s, drecv_s, cols, ex_send, ex_recv, ex_all, load) = refs[57:]
    (send_rows, grid_lat, w_grid_send, mesh_lat, recv_rows, feat, w_grid_recv, w_grid_out, w_feat, gain_grid, w_node_in,
     w_node_out, gain_node, w_proc_send, w_proc_recv, halo_rows, from_row, to_row, w_proc_out, gain_proc, w_upd_in, w_upd_out,
     gain_upd, cot) = held
    loads = [pltpu.make_async_copy(stored[n], held[n], load.at[n]) for n in range(24)]
    for copy in loads[:6]:
        copy.start()
    me = coordinates()
    barrier, greeted = greet([offset_peer(k, 1) for k in range(9) if k != OWN] + [core_peer(me)] + [ring_peer(me, d, s) for d in range(3) for s in (1, 2, 3)])

    def mesh_copy(k):
        return push(mesh_lat, mesh_in.at[k], ex_send.at[0], ex_recv.at[0, k], offset_peer(k, -1))

    def index_copy(k):
        return push(recv_rows.at[k], index_in.at[k], ex_send.at[1], ex_recv.at[1, k], offset_peer(k, -1))

    def feat_copy(k):
        return push(feat.at[k], feat_in.at[k], ex_send.at[2], ex_recv.at[2, k], offset_peer(k, -1))

    def part_copy(k):
        return push(part_out.at[k], part_in.at[k], ex_send.at[4], ex_all.at[0], offset_peer(k, 1))

    def dsum_copy(k):
        return push(dsum_out, dsum_in.at[k], ex_send.at[3], ex_recv.at[3, k], offset_peer(k, -1))

    ways = ((1, 0), (-1, 0), (0, 1), (0, -1))

    def halo_copy(j):
        return push(halo_out.at[pl.ds(16 * j, 16)], table.at[pl.ds(64 + 16 * j, 16)], ex_send.at[5], ex_all.at[1], tile_peer(*ways[j]))

    def back_copy(j):
        dlat, dlon = ways[j]
        return push(back_out.at[pl.ds(16 * j, 16)], back_in.at[pl.ds(16 * j, 16)], ex_send.at[6], ex_all.at[2], tile_peer(-dlat, -dlon))

    def landed(ref, n):
        push(ref, ref, ex_send.at[0], ex_all.at[n], core_peer(me)).wait_recv()

    def each(copy):
        for k in REMOTE:
            copy(k).start()

    for copy in loads[:3]:
        copy.wait()
    padded = jnp.concatenate([send_rows[k] for k in range(9)] + [jnp.zeros((7, 256), jnp.int32)], axis=0).astype(F32)
    cols[...] = jnp.transpose(padded)

    def slots_body(k, carry):
        lane = lax.broadcasted_iota(jnp.int32, (256, 16), 1)
        col = jnp.sum(jnp.where(lane == k, cols[...], 0.0), axis=1, keepdims=True).astype(jnp.int32)
        pick = (col == lax.broadcasted_iota(jnp.int32, (256, 1024), 1)).astype(F32).astype(BF)
        x = mm(pick, grid_lat[...]).astype(BF)
        x_s[k] = x
        slots[k] = mm(x, w_grid_send[...]).astype(BF)
        return carry

    lax.fori_loop(0, 3, slots_body, 0)
    for copy in loads[3:6]:
        copy.wait()
    pl.semaphore_wait(barrier, greeted)
    each(index_copy)
    each(feat_copy)
    each(mesh_copy)
    for copy in loads[6:]:
        copy.start()
    mesh_in[OWN] = mesh_lat[...]
    index_in[OWN] = recv_rows[OWN]
    feat_in[OWN] = feat[OWN]
    lax.fori_loop(3, 9, slots_body, 0)
    for copy in loads[6:10]:
        copy.wait()

    def receivers(k):
        return (index_in[k] == lax.broadcasted_iota(jnp.int32, (64, 256), 0)).astype(F32).astype(BF)

    near, far = 5 - 2 * me[3], 3 + 2 * me[3]
    order = (near, far, 1, 7, 0, 6, 2, 8)

    def forward(k):
        if k is not OWN:
            mesh_copy(k).wait_recv()
            index_copy(k).wait_recv()
            feat_copy(k).wait_recv()
        full_terms = mm(mesh_in[k], w_grid_recv[...])
        high = full_terms.astype(BF)
        low = (full_terms - high.astype(F32)).astype(BF)
        rec = receivers(k)
        left = jnp.concatenate([rec, rec, feat_in[k], jnp.zeros((12, 256), BF)], axis=0)
        right = jnp.concatenate([high, low, w_feat[...], jnp.zeros((12, 512), BF)], axis=0)
        pre = slots[k].astype(F32) + mm_t(left, right)
        hid, zhat, inv, slope = tail_forward(pre, w_grid_out[...])
        hid_s[k], zhat_s[k], slope_s[k] = hid, zhat.astype(BF), slope.astype(BF)
        inv_s[k] = inv
        part_out[k] = (mm(rec, zhat.astype(BF)) * gain_grid[...]).astype(BF)
        if k is not OWN:
            part_copy(k).start()

    for k in order + (OWN,):
        forward(k)

    for copy in loads[10:]:
        copy.wait()
    node_pre = mm(mesh_lat[...], w_node_in[:512, :])
    grid_sum = part_out[OWN].astype(F32)
    landed(part_in.at[pl.ds(0, 8)], 0)
    for k in REMOTE:
        grid_sum = grid_sum + part_in[k].astype(F32)
    node_pre = node_pre + mm(grid_sum.astype(BF), w_node_in[512:, :])
    node_hid, node_zhat, node_inv, node_slope = tail_forward(node_pre, w_node_out[...])
    state = mesh_lat[...].astype(F32) + node_zhat * gain_node[...]
    state_bf = state.astype(BF)
    own_terms = mm(state_bf, w_proc_send[...]).astype(BF)
    spots = lax.broadcasted_iota(jnp.int32, (64, 16), 0)
    lists = [(halo_rows[j : j + 1, :] == spots).astype(F32).astype(BF) for j in range(4)]
    for j in range(4):
        halo_out[pl.ds(16 * j, 16), :] = mm_t(lists[j], own_terms).astype(BF)
        halo_copy(j).start()
    table[:64, :] = own_terms
    p_recv = mm(state_bf, w_proc_recv[...])
    p_high = p_recv.astype(BF)
    p_low = (p_recv - p_high.astype(F32)).astype(BF)
    pick_from = (from_row[...] == lax.broadcasted_iota(jnp.int32, (128, 512), 0)).astype(F32).astype(BF)
    pick_to = (to_row[...] == lax.broadcasted_iota(jnp.int32, (64, 512), 0)).astype(F32).astype(BF)
    upd_pre = mm(state_bf, w_upd_in[:512, :])
    landed(table.at[pl.ds(64, 64)], 1)
    left = jnp.concatenate([pick_from, pick_to, pick_to], axis=0)
    right = jnp.concatenate([table[...], p_high, p_low], axis=0)
    proc_pre = mm_t(left, right)
    p_hid, p_zhat, p_inv, p_slope = tail_forward(proc_pre, w_proc_out[...])
    proc_sum = mm(pick_to, p_zhat.astype(BF)) * gain_proc[...]
    upd_pre = upd_pre + mm(proc_sum.astype(BF), w_upd_in[512:, :])
    upd_hid, upd_zhat, upd_inv, upd_slope = tail_forward(upd_pre, w_upd_out[...])
    mesh_out[...] = state + upd_zhat * gain_upd[...]
    top = cot[...].astype(F32)
    d_upd = tail_backward(top, gain_upd[...], upd_zhat, upd_inv, upd_slope, w_upd_out[...])[1].astype(BF)
    d_sum = mm_nt(d_upd, w_upd_in[512:, :])
    d_state = top + mm_nt(d_upd, w_upd_in[:512, :])
    d_msg = mm_t(pick_to, d_sum.astype(BF))
    dz, d_pre = tail_backward(d_msg, gain_proc[...], p_zhat, p_inv, p_slope, w_proc_out[...])
    d_pre = d_pre.astype(BF)
    d_table = mm(pick_from, d_pre)
    back_out[...] = d_table[64:, :].astype(BF)
    for j in range(4):
        back_copy(j).start()
    d_recv2 = mm(pick_to, d_pre).astype(BF)
    d_state = d_state + mm_nt(d_recv2, w_proc_recv[...])
    grads[3] = mm_t(p_hid, dz)
    grads[4] = mm_t(state_bf, d_recv2)
    landed(back_in, 2)
    d_own = d_table[:64, :]
    for j in range(4):
        d_own = d_own + mm(lists[j], back_in[pl.ds(16 * j, 16), :])
    d_own = d_own.astype(BF)
    d_state = d_state + mm_nt(d_own, w_proc_send[...])
    d_node = tail_backward(d_state, gain_node[...], node_zhat, node_inv, node_slope, w_node_out[...])[1].astype(BF)
    dsum_out[...] = mm_nt(d_node, w_node_in[512:, :]).astype(BF)
    each(dsum_copy)
    dsum_in[OWN] = dsum_out[...]
    grads[5] = mm_t(state_bf, d_own)
    parts = []
    for n in range(12):
        g, half = n // 2, n % 2
        bufs = [b.at[n] for b in red] + [full.at[g, half]]
        parts.append(Reduction(g % 3, grads.at[g, pl.ds(256 * half, 256)], bufs, red_send.at[n], red_recv.at[n], red[2].at[pl.ds(0, 5)]))
    early = parts[6:]
    for part in early:
        part.begin()

    grads[0] = jnp.zeros((512, 512), F32)
    grads[2] = jnp.zeros((512, 512), F32)
    def backward(k):
        if k is not OWN:
            dsum_copy(k).wait_recv()
        rec = receivers(k)
        grad = mm_t(rec, dsum_in[k])
        zhat = zhat_s[k].astype(F32)
        dz, dpre = tail_backward(grad, gain_grid[...], zhat, inv_s[k], slope_s[k].astype(F32), w_grid_out[...])
        grads[2] += mm_t(hid_s[k], dz)
        dpre = dpre.astype(BF)
        dpre_s[k] = dpre
        grads[0] += mm_t(x_s[k], dpre)
        drecv_s[k] = mm(rec, dpre).astype(BF)

    for n, k in enumerate((OWN,) + order):
        backward(k)
        if n == 3:
            for part in early:
                part.stage(0)
    late = (parts[4], parts[0], parts[5], parts[1], parts[2], parts[3])
    for part in late[:4]:
        part.begin()
    grads[1] = mm_t(mesh_in[...].reshape(576, 512), drecv_s[...].reshape(576, 512))
    for part in late[4:]:
        part.begin()
    every = jnp.concatenate([send_rows[k] for k in range(9)], axis=1)

    def terms_back(i, carry):
        rows = pl.ds(pl.multiple_of(i * 256, 256), 256)
        ids = lax.broadcasted_iota(jnp.int32, (256, 2304), 0) + i * 256
        put = (every == ids).astype(F32).astype(BF)
        d_terms[rows, :] = mm(put, dpre_s[...].reshape(2304, 512)).astype(BF)
        return carry

    def run(group, level):
        for part in group:
            part.stage(level)

    run(late, 0)
    run(early, 1)
    lax.fori_loop(0, 2, terms_back, 0)
    run(early, 2)
    run(late, 1)
    lax.fori_loop(2, 3, terms_back, 0)
    run(early, 3)
    run(late, 2)
    lax.fori_loop(3, 4, terms_back, 0)
    run(early, 4)
    run(late, 3)
    run(late, 4)
    for part in early:
        part.finish()
    for part in late:
        part.finish()
    sent = (mesh_in, index_in, feat_in, dsum_in, part_in)
    for n, ref in enumerate([r.at[pl.ds(0, 8)] for r in sent] + [table.at[pl.ds(0, 64)], back_in]):
        push(ref, ref, ex_send.at[n], ex_all.at[0], core_peer(me)).wait_send()


def finish_kernel(full, d_terms, mesh_in, w_grid_send, *refs):
    outs, (weight_v, out_v, grid_v, in_sem, out_sem) = refs[:8], refs[8:]
    load = pltpu.make_async_copy(w_grid_send, weight_v, in_sem)
    load.start()
    done = [pltpu.make_async_copy(mesh_in, outs[7], out_sem.at[10])]
    done[0].start()
    for g in range(6):

        def spread(i, carry, g=g):
            out_v[g, pl.ds(pl.multiple_of(i * 32, 32), 32), :] = full[g, i // 8, lax.rem(i // 4, 2), lax.rem(i, 4)].astype(F32)
            return carry

        lax.fori_loop(0, 16, spread, 0)
        done.append(pltpu.make_async_copy(out_v.at[g], outs[g], out_sem.at[g]))
        done[-1].start()
        if g == 1:
            load.wait()
        if g >= 1 and g < 5:
            rows = pl.ds(256 * (g - 1), 256)
            grid_v[rows, :] = mm_nt(d_terms[rows, :], weight_v[...])
            done.append(pltpu.make_async_copy(grid_v.at[rows], outs[6].at[rows], out_sem.at[5 + g]))
            done[-1].start()
    for copy in done:
        copy.wait()


def local(
    grid_lat,
    mesh_lat,
    g2m_send,
    g2m_recv,
    g2m_feat,
    halo_lists,
    proc_send,
    proc_recv,
    cotangent,
    w_grid_send,
    w_grid_recv,
    w_grid_feat,
    w_grid_out,
    gain_grid,
    w_node_in,
    w_node_out,
    gain_node,
    w_proc_send,
    w_proc_recv,
    w_proc_out,
    gain_proc,
    w_upd_in,
    w_upd_out,
    gain_upd,
):
    feat = g2m_feat[0].reshape(4, 9, 256).transpose(1, 0, 2)
    send_rows = g2m_send.transpose(1, 0, 2)
    recv_rows = g2m_recv.transpose(1, 0, 2)
    row = lambda gain: gain.reshape(1, 512)
    vmem = pl.BlockSpec(memory_space=pltpu.VMEM)
    dma = pltpu.SemaphoreType.DMA
    block = lambda *shape: pltpu.VMEM(shape, BF)
    given = (
        send_rows, grid_lat, w_grid_send, mesh_lat, recv_rows, feat, w_grid_recv, w_grid_out, w_grid_feat, row(gain_grid),
        w_node_in, w_node_out, row(gain_node), w_proc_send, w_proc_recv, halo_lists[0], proc_send, proc_recv, w_proc_out,
        row(gain_proc), w_upd_in, w_upd_out, row(gain_upd), cotangent,
    )
    full, d_terms, mesh_new = pl.pallas_call(
        main_kernel,
        out_shape=[
            pltpu.VMEM((6, 2, 2, 4, 32, 512), BF),
            pltpu.VMEM((1024, 512), BF),
            pltpu.VMEM((64, 512), F32),
        ],
        in_specs=[pl.BlockSpec(memory_space=pl.ANY)] * 24,
        out_specs=[vmem] * 3,
        scratch_shapes=reduction_scratch(12)
        + [pltpu.VMEM(value.shape, value.dtype) for value in given]
        + [
            dma((12,)),
            dma((12, 6)),
            pltpu.VMEM((6, 512, 512), F32),
            block(9, 64, 512),
            pltpu.VMEM((9, 1, 256), jnp.int32),
            block(9, 4, 256),
            block(9, 64, 512),
            block(9, 64, 512),
            block(64, 512),
            block(9, 64, 512),
            block(64, 512),
            block(128, 512),
            block(64, 512),
            block(64, 512),
            block(9, 256, 512),
            block(9, 256, 512),
            block(9, 256, 512),
            block(9, 256, 512),
            block(9, 256, 512),
            pltpu.VMEM((9, 256, 1), F32),
            block(9, 256, 512),
            block(9, 64, 512),
            pltpu.VMEM((256, 16), F32),
            dma((7,)),
            dma((4, 9)),
            dma((3,)),
            dma((24,)),
        ],
        compiler_params=pltpu.CompilerParams(collective_id=0, has_side_effects=True, vmem_limit_bytes=59 << 20),
        name="step",
    )(*given)
    outs = pl.pallas_call(
        finish_kernel,
        out_shape=[jax.ShapeDtypeStruct((512, 512), F32)] * 6
        + [jax.ShapeDtypeStruct((1024, 512), F32), jax.ShapeDtypeStruct((64, 512), F32)],
        in_specs=[vmem] * 3 + [pl.BlockSpec(memory_space=pl.ANY)],
        out_specs=[pl.BlockSpec(memory_space=pl.ANY)] * 8,
        scratch_shapes=[
            block(512, 512),
            pltpu.VMEM((6, 512, 512), F32),
            pltpu.VMEM((1024, 512), F32),
            dma,
            dma((11,)),
        ],
        compiler_params=pltpu.CompilerParams(vmem_limit_bytes=40 << 20),
        name="finish",
    )(full, d_terms, mesh_new, w_grid_send)
    grid_send, grid_recv, grid_out, proc_out, proc_recv_g, proc_send_g, grid_grad, mesh_final = outs
    return mesh_final, grid_grad, grid_send, grid_recv, grid_out, proc_send_g, proc_recv_g, proc_out


def solution(mesh):
    placed = (
        P(("lat", "lon"), None),
        P(("lat", "lon"), None),
        P(("lat", "lon"), None, None),
        P(("lat", "lon"), None, None),
        P(("lat", "lon"), None, None),
        P(("lat", "lon"), None, None),
        P(("lat", "lon"), None),
        P(("lat", "lon"), None),
        P(("lat", "lon"), None),
        P(),
        P(),
        P(),
        P(),
        P(),
        P(),
        P(),
        P(),
        P(),
        P(),
        P(),
        P(),
        P(),
        P(),
        P(),
    )
    return jax.shard_map(
        local,
        mesh=mesh,
        in_specs=placed,
        out_specs=(P(("lat", "lon"), None), P(("lat", "lon"), None), P(), P(), P(), P(), P(), P()),
        check_vma=False,
    )
```
